512 devices in a mesh: tile: 8 (over x, core), beam: 64 (over y, z).
Axes of the slice: x: 4, y: 4, z: 16, core: 2. Of those that a mesh axis runs over, the one named last changes fastest.
Arguments:
- echoes: bfloat16 [2, 2048, 32768], P(None, 'tile', 'beam'), may hold values from -160 to 160
- steer: bfloat16 [2, 2048, 2048], P(None, None, 'tile'), may hold values from -0.09375 to 0.09375
- code: bfloat16 [2, 8], replicated, may hold values from -1 to 1
- beam_order: int32 [2048], replicated, may hold values from 0 to 2047, each once
- dwell: int32 [2048], replicated, may hold values from 256 to 1024, as said below
- code_len: int32 [2048], replicated, may hold values from 1 to 8, as said below
Outputs:
- spectrum: float32 [2048, 2, 32, 1024], P(('tile', 'beam'))
The draws below stay inside these ranges and needn't reach their ends.
Inputs may be any that keep to these rules, and one draw needn't show every extreme that they name: dwell[b] counts the leading pulses that beam b keeps; some beam keeps all 1024. `code_len`: some beam uses all 8 taps.
All inputs are finite; a program needn't handle non-finite values.
Results may differ from the reference program's by a relative error of at most 0.015.
Values may be sent and summed in bfloat16 or wider, within the bound.
A program may use at most 64 MiB of HBM per device.

```python
import math
import jax
import jax.numpy as jnp
from jax import lax

C = 2048
B = 2048
G = 32
CODE = 8
P_SIZE = 1024
N_TILE = 8


def draw_echoes(key, part):
    key_data, key_chan = jax.random.split(jax.random.fold_in(key, 3))
    chan = jnp.exp(jax.random.uniform(key_chan, (C,), jnp.float32) * math.log(10.0))
    ramp = jnp.arange(P_SIZE, dtype=jnp.float32) / max(P_SIZE - 1, 1)
    amp = jnp.exp(ramp * math.log(3.0))
    base = jnp.clip(jax.random.normal(key_data, (2, C, P_SIZE, G), jnp.float32), -4.0, 4.0)
    values = base * chan[None, :, None, None] * amp[None, None, :, None]
    return values.reshape(2, C, P_SIZE * G).astype(jnp.bfloat16)


def draw_dwell(key, part):
    key_vals, key_at = jax.random.split(jax.random.fold_in(key, 11))
    vals = jax.random.randint(key_vals, (B,), P_SIZE // 4, P_SIZE + 1)
    where = jax.random.randint(key_at, (), 0, B)
    return vals.at[where].set(P_SIZE)


def draw_code_len(key, part):
    key_vals, key_at = jax.random.split(jax.random.fold_in(key, 17))
    vals = jax.random.randint(key_vals, (B,), 1, CODE + 1)
    where = jax.random.randint(key_at, (), 0, B)
    return vals.at[where].set(CODE)


def levels(rng, shape, cuts, low, top_value):
    def one(axis_at, parts):
        heights = jax.random.uniform(jax.random.fold_in(jax.random.fold_in(rng, 6), axis_at), (parts,), jnp.float32, low / len(cuts), top_value / len(cuts))
        return jnp.repeat(jnp.exp(heights), shape[axis_at] // parts).reshape((-1,) + (1,) * (len(shape) - axis_at - 1))

    factor_of = one(*cuts[0])
    for cut in cuts[1:]:
        factor_of = factor_of * one(*cut)
    return factor_of


def normal_values(stream_key, dims, deviation, limit, shards=(), kind=jnp.bfloat16):
    factor_of = levels(stream_key, dims, shards, -0.22, 0.18) if shards else 1.0
    drawn = jax.random.normal(stream_key, dims, jnp.float32) * deviation * factor_of
    return jnp.minimum(jnp.maximum(drawn, -limit), limit).astype(kind)


def setup_inputs(seed: int = 0) -> dict:
    streams_of = jax.random.split(jax.random.key(seed), 7)
    echoes = draw_echoes(jax.random.fold_in(streams_of[6], 71), 0)
    steer = normal_values(streams_of[1], (2, B, C), (2 * C) ** -0.5, 0.09375, ((2, 8),))
    code = normal_values(streams_of[2], (2, CODE), 0.25, 1.0)
    beam_order = jax.random.permutation(streams_of[3], B).astype(jnp.int32)
    dwell = draw_dwell(jax.random.fold_in(streams_of[6], 71), 0)
    code_len = draw_code_len(jax.random.fold_in(streams_of[6], 71), 0)
    return dict(echoes=echoes, steer=steer, code=code, beam_order=beam_order, dwell=dwell, code_len=code_len)


def complex_block(weight_re, weight_im):
    upper = jnp.concatenate([weight_re, -weight_im], axis=1)
    lower = jnp.concatenate([weight_im, weight_re], axis=1)
    return jnp.stack([upper, lower], axis=1).reshape(2 * weight_re.shape[0], 2 * weight_re.shape[1])

def dft_rows(first, count, total):
    row_index = first + jnp.arange(count, dtype=jnp.int32)
    freqs = jnp.arange(total, dtype=jnp.int32)
    phase = row_index[:, None] * freqs[None, :] % total
    angle = phase.astype(jnp.float32) * (2.0 * math.pi / total)
    return (jnp.cos(angle), -jnp.sin(angle))

def compress(values, code, lens, limits, first_pulse):
    gates = values.shape[3]
    taps = code.shape[1]
    padded = jnp.pad(values, ((0, 0), (0, 0), (0, 0), (0, taps)))
    code_re = code[0].astype(jnp.float32)
    code_im = code[1].astype(jnp.float32)
    out_re = jnp.zeros((values.shape[0], values.shape[2], gates), jnp.float32)
    out_im = jnp.zeros((values.shape[0], values.shape[2], gates), jnp.float32)
    for tap in range(taps):
        live = (tap < lens).astype(jnp.float32)[:, None, None]
        shift_re = padded[:, 0, :, tap:tap + gates]
        shift_im = padded[:, 1, :, tap:tap + gates]
        out_re = out_re + live * (code_re[tap] * shift_re + code_im[tap] * shift_im)
        out_im = out_im + live * (code_re[tap] * shift_im - code_im[tap] * shift_re)
    pulse_index = first_pulse + jnp.arange(values.shape[2], dtype=jnp.int32)
    keep = (pulse_index[None, :] < limits[:, None]).astype(jnp.float32)[:, None, :, None]
    return (jnp.stack([out_re, out_im], axis=1) * keep).astype(jnp.bfloat16)

def reference(echoes, steer, code, beam_order, dwell, code_len):
    beam_total = steer.shape[1]
    chans = C // N_TILE
    columns = P_SIZE * G
    values = echoes.astype(jnp.float32)
    power = lax.optimization_barrier(jnp.sum(values * values, axis=(0, 2))) / (P_SIZE * G)
    gain = lax.rsqrt(power + 1e-05)
    ordered = jnp.take(steer, beam_order, axis=1)
    weights = (ordered.astype(jnp.float32) * gain).astype(jnp.bfloat16)
    blocks = [complex_block(weights[0, :, t * chans:(t + 1) * chans], weights[1, :, t * chans:(t + 1) * chans]) for t in range(N_TILE)]
    width = min(512, columns)
    count = columns // width

    def beam_cols(index):
        part = lax.dynamic_slice_in_dim(echoes, index * width, width, 2)
        total = jnp.zeros((beam_total, 2, width), jnp.float32)
        for t in range(N_TILE):
            flat = part[:, t * chans:(t + 1) * chans, :].reshape(2 * chans, width)
            term = jnp.dot(blocks[t], flat, preferred_element_type=jnp.float32).reshape(beam_total, 2, width)
            total = total + lax.optimization_barrier(term.astype(jnp.bfloat16)).astype(jnp.float32)
        return total.astype(jnp.bfloat16)
    pieces = lax.map(beam_cols, jnp.arange(count, dtype=jnp.int32))
    beams = jnp.transpose(pieces, (1, 2, 0, 3)).reshape(beam_total, 2, P_SIZE, G)
    lens = jnp.take(code_len, beam_order)
    limits = jnp.take(dwell, beam_order)
    table_re, table_im = dft_rows(0, P_SIZE, P_SIZE)
    group = min(64, beam_total)
    groups = beam_total // group

    def per_group(inputs):
        beam_part, lens_part, limits_part = inputs
        squeezed = compress(beam_part.astype(jnp.float32), code, lens_part, limits_part, 0).astype(jnp.float32)
        first = jnp.einsum('bcpg,pk->bcgk', squeezed, table_re, precision=lax.Precision.HIGHEST)
        second = jnp.einsum('bcpg,pk->bcgk', squeezed, table_im, precision=lax.Precision.HIGHEST)
        joined = jnp.stack([first[:, 0] - second[:, 1], first[:, 1] + second[:, 0]], axis=1)
        return joined * (1.0 / math.sqrt(P_SIZE))
    result = lax.map(per_group, (beams.reshape(groups, group, 2, P_SIZE, G), lens.reshape(groups, group), limits.reshape(groups, group)))
    return result.reshape(beam_total, 2, G, P_SIZE)
```

```python
import math

import jax
import jax.numpy as jnp
import numpy as np
from jax import lax
from jax.experimental import pallas as pl
from jax.experimental.pallas import tpu as pltpu
from jax.sharding import PartitionSpec as P

G = 32
TAPS = 8
LANES = 128
MESH = pl.DeviceIdType.MESH
F32 = jnp.float32
BF16 = jnp.bfloat16


def exchange_kernel(
    nb,
    echo_hbm, steer_hbm, order_ref, dwell_ref, lens_ref, code_ref,
    out_ref,
    echo, steer, cols, perm, perm_out, power, gains, limit, pulses, rhs, xsend, own, xrecv, weave, zsend,
    local_sem, ar_send, ar_recv, pair_send, pair_recv, x_send, x_recv, z_send, z_recv, self_sem,
):
    nz = min(16, nb)
    ny = nb // nz
    tile = lax.axis_index("tile")
    beam = lax.axis_index("beam")
    core = lax.rem(tile, 2)
    chip_x = tile // 2
    partner = tile + 1 - 2 * core
    my_y = beam // nz
    my_z = lax.rem(beam, nz)
    chans = echo.shape[2]
    chunks = zsend.shape[0]
    slots = perm.shape[2]
    rows_total = steer.shape[1]
    blocks = rows_total // LANES
    half_blocks = slots // LANES
    nlane = chans // LANES

    def plane_peer(i):
        k = (nb - 1 - i) // ny
        dy = lax.rem(nb - 1 - i, ny)
        sign = 1 - 2 * lax.rem(k + 1, 2)
        dz = sign * ((k + 1) // 2)
        return lax.rem(my_y + dy, ny) * nz + lax.rem(my_z + dz + nz, nz)

    get_echo = pltpu.make_async_copy(echo_hbm, echo.at[core], local_sem.at[0])
    get_steer = pltpu.make_async_copy(steer_hbm, steer, local_sem.at[1])
    get_echo.start()
    get_steer.start()

    barrier = pltpu.get_barrier_semaphore()

    @pl.loop(0, nb - 1)
    def _(i):
        pl.semaphore_signal(barrier, inc=1, device_id={"beam": plane_peer(i)}, device_id_type=MESH)

    x_peers = [2 * lax.rem(chip_x + d, 4) + core for d in (2, 1, 3)]
    for peer in x_peers + [partner]:
        pl.semaphore_signal(barrier, inc=1, device_id={"tile": peer}, device_id_type=MESH)

    order_cols = order_ref[...].astype(F32)
    lane = lax.broadcasted_iota(jnp.int32, (LANES, LANES), 1)
    for b in range(blocks):
        cols[b] = jnp.broadcast_to(order_cols[b : b + 1, :], (LANES, LANES)).T

    get_echo.wait()
    for v in range(nlane):
        total = jnp.zeros((LANES, LANES), F32)
        for c in range(2):
            for q in range(chunks):
                part = echo[core, c, v * LANES : (v + 1) * LANES, q * LANES : (q + 1) * LANES].astype(F32)
                total = total + part * part
        power[beam, v : v + 1, :] = jnp.sum(total.T, axis=0, keepdims=True)

    lane_f = lane.astype(F32)

    def one_hot_block(b):
        col = cols[b]
        return [(col == lane_f + float(w * LANES)) for w in range(blocks)]

    def permuted(b):
        hot = jnp.concatenate([m.astype(F32).astype(BF16) for m in one_hot_block(b)], axis=1)
        left = jnp.dot(hot, steer[0], preferred_element_type=F32)
        right = jnp.dot(hot, steer[1], preferred_element_type=F32)
        return left.astype(BF16), right.astype(BF16)

    for u in range(half_blocks):
        masks = one_hot_block(tile * half_blocks + u)
        length = jnp.zeros((LANES, LANES), F32)
        keep = jnp.zeros((LANES, LANES), F32)
        for w in range(blocks):
            length = length + jnp.where(masks[w], lens_ref[w : w + 1, :].astype(F32), 0.0)
            keep = keep + jnp.where(masks[w], dwell_ref[w : w + 1, :].astype(F32), 0.0)
        length = jnp.sum(length, axis=1, keepdims=True)
        keep = jnp.sum(keep, axis=1, keepdims=True)
        gate = lax.rem(lane, G).astype(F32)
        limit[u * LANES : (u + 1) * LANES, :] = jnp.minimum(jnp.broadcast_to(length, (LANES, LANES)), G - gate)
        first = (lane // G + beam * (chunks * (LANES // G))).astype(F32)
        pulses[u * LANES : (u + 1) * LANES, :] = jnp.broadcast_to(keep, (LANES, LANES)) - first

    get_steer.wait()

    @pl.loop(0, 4 * half_blocks)
    def _(i):
        dest = i // half_blocks
        u = lax.rem(i, half_blocks)
        left, right = permuted((dest * 2 + core) * half_blocks + u)
        perm[core, dest, pl.ds(pl.multiple_of(u * LANES, LANES), LANES), :chans] = left
        perm[core, dest, pl.ds(pl.multiple_of(u * LANES, LANES), LANES), chans:] = right

    pl.semaphore_wait(barrier, nb - 1 + 4)

    @pl.loop(0, nb - 1)
    def _(i):
        pltpu.make_async_remote_copy(
            power.at[beam], power.at[beam], ar_send, ar_recv,
            device_id={"beam": plane_peer(i)}, device_id_type=MESH,
        ).start()

    send_echo = pltpu.make_async_remote_copy(
        echo.at[core], echo.at[core], pair_send.at[0], pair_recv.at[0],
        device_id={"tile": partner}, device_id_type=MESH,
    )
    send_echo.start()

    @pl.loop(0, 4 * half_blocks)
    def _(i):
        dest = i // half_blocks
        u = lax.rem(i, half_blocks)
        left, right = permuted((dest * 2 + 1 - core) * half_blocks + u)
        perm_out[dest, pl.ds(pl.multiple_of(u * LANES, LANES), LANES), :chans] = left
        perm_out[dest, pl.ds(pl.multiple_of(u * LANES, LANES), LANES), chans:] = right

    send_perm = pltpu.make_async_remote_copy(
        perm_out, perm.at[core], pair_send.at[1], pair_recv.at[1],
        device_id={"tile": partner}, device_id_type=MESH,
    )
    send_perm.start()

    everyone = power.at[pl.ds(0, nb - 1)]
    pltpu.make_async_copy(everyone, everyone, ar_recv).wait()
    summed = jnp.sum(power[...], axis=0)
    gains[core] = lax.rsqrt(summed * (1.0 / (nb * chunks * LANES)) + 1e-05)
    send_gain = pltpu.make_async_remote_copy(
        gains.at[core], gains.at[core], pair_send.at[2], pair_recv.at[2],
        device_id={"tile": partner}, device_id_type=MESH,
    )
    send_gain.start()

    def scale_side(side):
        for v in range(nlane):
            gain = jnp.broadcast_to(gains[side, v : v + 1, :], (LANES, LANES)).T
            top = slice(v * LANES, (v + 1) * LANES)
            low = slice(chans + v * LANES, chans + (v + 1) * LANES)
            for q in range(chunks):
                span = slice(q * LANES, (q + 1) * LANES)
                real = (echo[side, 0, top, span].astype(F32) * gain).astype(BF16)
                imag = (echo[side, 1, top, span].astype(F32) * gain).astype(BF16)
                rhs[q, side, top, :LANES] = real
                rhs[q, side, low, :LANES] = -imag
                rhs[q, side, top, LANES:] = imag
                rhs[q, side, low, LANES:] = real

    scale_side(core)
    send_echo.wait_recv()
    send_gain.wait_recv()
    scale_side(1 - core)
    send_perm.wait_recv()

    def partial_beams(q, dest):
        return jnp.dot(perm[0, dest], rhs[q, 0], preferred_element_type=F32) + jnp.dot(
            perm[1, dest], rhs[q, 1], preferred_element_type=F32
        )

    x_copies = []
    for q in range(chunks):
        for s, peer in enumerate(x_peers):
            xsend[q, s] = partial_beams(q, peer // 2).astype(BF16)
            copy = pltpu.make_async_remote_copy(
                xsend.at[q, s], xrecv.at[q, s], x_send.at[q, s], x_recv.at[q, s],
                device_id={"tile": peer}, device_id_type=MESH,
            )
            copy.start()
            x_copies.append(copy)
        own[q] = partial_beams(q, chip_x)

    step = 64
    for q in range(chunks):
        for s in range(3):
            x_copies[3 * q + s].wait_recv()

        @pl.loop(0, slots // step)
        def _(r):
            rows = pl.ds(pl.multiple_of(r * step, step), step)
            both = own[q, rows, :]
            for s in range(3):
                both = both + xrecv[q, s, rows, :].astype(F32)
            real, imag = both[:, :LANES], both[:, LANES:]
            cut = limit[rows, :]
            out_re = jnp.zeros((step, LANES), F32)
            out_im = jnp.zeros((step, LANES), F32)
            for tap in range(TAPS):
                live = cut > float(tap)
                shift_re = real if tap == 0 else pltpu.roll(real, LANES - tap, 1)
                shift_im = imag if tap == 0 else pltpu.roll(imag, LANES - tap, 1)
                shift_re = jnp.where(live, shift_re, 0.0)
                shift_im = jnp.where(live, shift_im, 0.0)
                code_re = code_ref[0, tap]
                code_im = code_ref[1, tap]
                out_re = out_re + (code_re * shift_re + code_im * shift_im)
                out_im = out_im + (code_re * shift_im - code_im * shift_re)
            kept = pulses[rows, :] > float(q * (LANES // G))
            weave[pl.ds(r * (2 * step), step, stride=2), :] = jnp.where(kept, out_re, 0.0)
            weave[pl.ds(r * (2 * step) + 1, step, stride=2), :] = jnp.where(kept, out_im, 0.0)

        zsend[q] = weave[...].reshape(zsend.shape[1:]).astype(BF16)

        @pl.loop(0, nb - 1)
        def _(i):
            peer = plane_peer(i)
            pltpu.make_async_remote_copy(
                zsend.at[q, peer], out_ref.at[q, beam], z_send.at[q], z_recv.at[q],
                device_id={"beam": peer}, device_id_type=MESH,
            ).start()

        pltpu.make_async_copy(zsend.at[q, beam], out_ref.at[q, beam], self_sem.at[q]).start()

    for q in range(chunks):
        arrived = out_ref.at[q, pl.ds(0, nb - 1)]
        pltpu.make_async_copy(arrived, arrived, z_recv.at[q]).wait()
        pltpu.make_async_copy(zsend.at[q, beam], out_ref.at[q, beam], self_sem.at[q]).wait()

    pltpu.make_async_copy(everyone, everyone, ar_send).wait()
    send_echo.wait_send()
    send_perm.wait_send()
    send_gain.wait_send()
    for copy in x_copies:
        copy.wait_send()
    for q in range(chunks):
        sent = zsend.at[q, pl.ds(0, nb - 1)]
        pltpu.make_async_copy(sent, sent, z_send.at[q]).wait()


def exchange(nb, echoes, steer, code, beam_order, dwell, code_len):
    chans, columns = echoes.shape[1], echoes.shape[2]
    total = steer.shape[1]
    slots = total // 8
    chunks = columns // LANES
    rows = 2 * slots // nb
    blocks = total // LANES
    vmem = pl.BlockSpec(memory_space=pltpu.VMEM)
    hbm = pl.BlockSpec(memory_space=pl.ANY)
    dma = pltpu.SemaphoreType.DMA

    def body(*refs):
        exchange_kernel(nb, *refs)

    return pl.pallas_call(
        body,
        out_shape=jax.ShapeDtypeStruct((chunks, nb, rows, LANES), BF16),
        in_specs=[hbm, hbm, vmem, vmem, vmem, pl.BlockSpec(memory_space=pltpu.SMEM)],
        out_specs=vmem,
        scratch_shapes=[
            pltpu.VMEM((2, 2, chans, columns), BF16),
            pltpu.VMEM(steer.shape, BF16),
            pltpu.VMEM((blocks, LANES, LANES), F32),
            pltpu.VMEM((2, 4, slots, 2 * chans), BF16),
            pltpu.VMEM((4, slots, 2 * chans), BF16),
            pltpu.VMEM((nb, chans // LANES, LANES), F32),
            pltpu.VMEM((2, chans // LANES, LANES), F32),
            pltpu.VMEM((slots, LANES), F32),
            pltpu.VMEM((slots, LANES), F32),
            pltpu.VMEM((chunks, 2, 2 * chans, 2 * LANES), BF16),
            pltpu.VMEM((chunks, 3, slots, 2 * LANES), BF16),
            pltpu.VMEM((chunks, slots, 2 * LANES), F32),
            pltpu.VMEM((chunks, 3, slots, 2 * LANES), BF16),
            pltpu.VMEM((2 * slots, LANES), F32),
            pltpu.VMEM((chunks, nb, rows, LANES), BF16),
            dma((2,)), dma, dma, dma((3,)), dma((3,)),
            dma((chunks, 3)), dma((chunks, 3)), dma((chunks,)), dma((chunks,)), dma((chunks,)),
        ],
        compiler_params=pltpu.CompilerParams(
            collective_id=0, has_side_effects=True, vmem_limit_bytes=40 << 20
        ),
        name="exchange",
    )(
        echoes, steer,
        beam_order.reshape(blocks, LANES), dwell.reshape(blocks, LANES), code_len.reshape(blocks, LANES),
        code.astype(F32),
    )


def dft_tables(nb, chunks, pulses_all):
    length = nb * chunks
    radix = pulses_all // length
    index = (np.arange(nb)[None, :] * chunks + np.arange(chunks)[:, None]).reshape(-1)
    angle = -2.0 * np.pi * ((index[:, None] * np.arange(length)[None, :]) % length) / length
    real, imag = np.cos(angle), np.sin(angle)
    table = np.block([[real, imag], [-imag, real]])
    turn = -2.0 * np.pi * np.arange(radix)[:, None] * np.arange(length)[None, :] / pulses_all
    twist = np.concatenate([np.cos(turn), np.sin(turn)], axis=0) / math.sqrt(pulses_all)
    return jnp.asarray(table, BF16), jnp.asarray(twist, F32)


def dft_kernel(x_ref, table_ref, twist_ref, out_ref, wide):
    chunks, nb, rows, _ = x_ref.shape
    length = chunks * nb
    wide[...] = x_ref[...].astype(F32).reshape(wide.shape)
    for slot in range(rows // 2):
        real = wide[pl.ds(2 * slot, length, stride=rows), :].T.astype(BF16)
        imag = wide[pl.ds(2 * slot + 1, length, stride=rows), :].T.astype(BF16)
        left = jnp.concatenate([real, imag], axis=1)
        found = jnp.dot(left, table_ref[...], preferred_element_type=F32)
        re, im = [], []
        for p in range(4):
            fr = found[p * G : (p + 1) * G, :length]
            fi = found[p * G : (p + 1) * G, length:]
            wr = twist_ref[p : p + 1, :]
            wi = twist_ref[4 + p : 5 + p, :]
            re.append(fr * wr - fi * wi)
            im.append(fr * wi + fi * wr)
        even_re, even_im = re[0] + re[2], im[0] + im[2]
        odd_re, odd_im = re[0] - re[2], im[0] - im[2]
        side_re, side_im = re[1] + re[3], im[1] + im[3]
        turn_re, turn_im = re[1] - re[3], im[1] - im[3]
        parts = [
            (even_re + side_re, even_im + side_im),
            (odd_re + turn_im, odd_im - turn_re),
            (even_re - side_re, even_im - side_im),
            (odd_re - turn_im, odd_im + turn_re),
        ]
        for k, (a, b) in enumerate(parts):
            out_ref[slot, 0, :, k * length : (k + 1) * length] = a
            out_ref[slot, 1, :, k * length : (k + 1) * length] = b


def doppler(x, pulses_all):
    chunks, nb, rows, _ = x.shape
    table, twist = dft_tables(nb, chunks, pulses_all)
    vmem = pl.BlockSpec(memory_space=pltpu.VMEM)
    return pl.pallas_call(
        dft_kernel,
        out_shape=jax.ShapeDtypeStruct((rows // 2, 2, G, pulses_all), F32),
        in_specs=[vmem, vmem, vmem],
        out_specs=vmem,
        scratch_shapes=[pltpu.VMEM((chunks * nb * rows, LANES), F32)],
        name="doppler",
    )(x, table, twist)


def solution(mesh):
    nb = mesh.shape["beam"]

    def on_device(echoes, steer, code, beam_order, dwell, code_len):
        arrived = exchange(nb, echoes, steer, code, beam_order, dwell, code_len)
        return doppler(arrived, nb * echoes.shape[2] // G)

    placed = (P(None, "tile", "beam"), P(None, None, "tile"), P(), P(), P(), P())
    return jax.shard_map(
        on_device,
        mesh=mesh,
        in_specs=placed,
        out_specs=P(("tile", "beam"), None, None, None),
        check_vma=False,
    )
```

```python
import math

import jax
import jax.numpy as jnp
import numpy as np
from jax import lax
from jax.experimental import pallas as pl
from jax.experimental.pallas import tpu as pltpu
from jax.sharding import PartitionSpec as P

G = 32
TAPS = 8
LANES = 128
MESH = pl.DeviceIdType.MESH
F32 = jnp.float32
BF16 = jnp.bfloat16


def exchange_kernel(
    nb,
    echo_hbm, steer_hbm, order_hbm, dwell_hbm, lens_hbm, code_hbm,
    out_ref,
    order_ref, dwell_ref, lens_ref, code_ref, coef,
    echo, steer, cols, perm, perm_out, power, gains, limit, pulses, rhs, xsend, own, xrecv, weave, zsend,
    local_sem, ar_send, ar_recv, pair_send, pair_recv, x_send, x_recv, z_send, z_recv, self_sem,
):
    nz = min(16, nb)
    ny = nb // nz
    tile = lax.axis_index("tile")
    beam = lax.axis_index("beam")
    core = lax.rem(tile, 2)
    chip_x = tile // 2
    partner = tile + 1 - 2 * core
    my_y = beam // nz
    my_z = lax.rem(beam, nz)
    chans = echo.shape[2]
    chunks = zsend.shape[0]
    slots = perm.shape[2]
    rows_total = steer.shape[1]
    blocks = rows_total // LANES
    half_blocks = slots // LANES
    nlane = chans // LANES

    def plane_peer(i):
        k = (nb - 1 - i) // ny
        dy = lax.rem(nb - 1 - i, ny)
        sign = 1 - 2 * lax.rem(k + 1, 2)
        dz = sign * ((k + 1) // 2)
        return lax.rem(my_y + dy, ny) * nz + lax.rem(my_z + dz + nz, nz)

    get_echo = pltpu.make_async_copy(echo_hbm, echo.at[core], local_sem.at[0])
    get_steer = pltpu.make_async_copy(steer_hbm, steer, local_sem.at[1])
    small = [
        pltpu.make_async_copy(source, target, local_sem.at[2 + n])
        for n, (source, target) in enumerate(
            [(order_hbm, order_ref), (dwell_hbm, dwell_ref), (lens_hbm, lens_ref), (code_hbm, code_ref)]
        )
    ]
    for copy in small[:1]:
        copy.start()
    get_echo.start()
    get_steer.start()
    for copy in small[1:]:
        copy.start()

    barrier = pltpu.get_barrier_semaphore()

    @pl.loop(0, nb - 1)
    def _(i):
        pl.semaphore_signal(barrier, inc=1, device_id={"beam": plane_peer(i)}, device_id_type=MESH)

    x_peers = [2 * lax.rem(chip_x + d, 4) + core for d in (2, 1, 3)]
    for peer in x_peers + [partner]:
        pl.semaphore_signal(barrier, inc=1, device_id={"tile": peer}, device_id_type=MESH)

    small[0].wait()
    order_cols = order_ref[...].astype(F32)
    lane = lax.broadcasted_iota(jnp.int32, (LANES, LANES), 1)
    for b in range(blocks):
        cols[b] = jnp.broadcast_to(order_cols[b : b + 1, :], (LANES, LANES)).T

    get_echo.wait()
    for v in range(nlane):
        total = jnp.zeros((LANES, LANES), F32)
        for c in range(2):
            for q in range(chunks):
                part = echo[core, c, v * LANES : (v + 1) * LANES, q * LANES : (q + 1) * LANES].astype(F32)
                total = total + part * part
        power[beam, v : v + 1, :] = jnp.sum(total.T, axis=0, keepdims=True)

    lane_f = lane.astype(F32)

    def one_hot_block(b):
        col = cols[b]
        return [(col == lane_f + float(w * LANES)) for w in range(blocks)]

    def permuted(b):
        hot = jnp.concatenate([m.astype(F32).astype(BF16) for m in one_hot_block(b)], axis=1)
        left = jnp.dot(hot, steer[0], preferred_element_type=F32)
        right = jnp.dot(hot, steer[1], preferred_element_type=F32)
        return left.astype(BF16), right.astype(BF16)

    for copy in small[1:]:
        copy.wait()
    taps = code_ref[...].astype(F32)
    for tap in range(TAPS):
        for c in range(2):
            coef[2 * tap + c] = jnp.broadcast_to(taps[c : c + 1, tap : tap + 1], coef.shape[1:])

    for u in range(half_blocks):
        masks = one_hot_block(tile * half_blocks + u)
        length = jnp.zeros((LANES, LANES), F32)
        keep = jnp.zeros((LANES, LANES), F32)
        for w in range(blocks):
            length = length + jnp.where(masks[w], lens_ref[w : w + 1, :].astype(F32), 0.0)
            keep = keep + jnp.where(masks[w], dwell_ref[w : w + 1, :].astype(F32), 0.0)
        length = jnp.sum(length, axis=1, keepdims=True)
        keep = jnp.sum(keep, axis=1, keepdims=True)
        gate = lax.rem(lane, G).astype(F32)
        limit[u * LANES : (u + 1) * LANES, :] = jnp.minimum(jnp.broadcast_to(length, (LANES, LANES)), G - gate)
        first = (lane // G + beam * (chunks * (LANES // G))).astype(F32)
        pulses[u * LANES : (u + 1) * LANES, :] = jnp.broadcast_to(keep, (LANES, LANES)) - first

    get_steer.wait()

    @pl.loop(0, 4 * half_blocks)
    def _(i):
        dest = i // half_blocks
        u = lax.rem(i, half_blocks)
        left, right = permuted((dest * 2 + core) * half_blocks + u)
        perm[core, dest, pl.ds(pl.multiple_of(u * LANES, LANES), LANES), :chans] = left
        perm[core, dest, pl.ds(pl.multiple_of(u * LANES, LANES), LANES), chans:] = right

    pl.semaphore_wait(barrier, nb - 1 + 4)

    @pl.loop(0, nb - 1)
    def _(i):
        pltpu.make_async_remote_copy(
            power.at[beam], power.at[beam], ar_send, ar_recv,
            device_id={"beam": plane_peer(i)}, device_id_type=MESH,
        ).start()

    send_echo = pltpu.make_async_remote_copy(
        echo.at[core], echo.at[core], pair_send.at[0], pair_recv.at[0],
        device_id={"tile": partner}, device_id_type=MESH,
    )
    send_echo.start()

    @pl.loop(0, 4 * half_blocks)
    def _(i):
        dest = i // half_blocks
        u = lax.rem(i, half_blocks)
        left, right = permuted((dest * 2 + 1 - core) * half_blocks + u)
        perm_out[dest, pl.ds(pl.multiple_of(u * LANES, LANES), LANES), :chans] = left
        perm_out[dest, pl.ds(pl.multiple_of(u * LANES, LANES), LANES), chans:] = right

    send_perm = pltpu.make_async_remote_copy(
        perm_out, perm.at[core], pair_send.at[1], pair_recv.at[1],
        device_id={"tile": partner}, device_id_type=MESH,
    )
    send_perm.start()

    everyone = power.at[pl.ds(0, nb - 1)]
    pltpu.make_async_copy(everyone, everyone, ar_recv).wait()
    summed = jnp.sum(power[...], axis=0)
    gains[core] = lax.rsqrt(summed * (1.0 / (nb * chunks * LANES)) + 1e-05)
    send_gain = pltpu.make_async_remote_copy(
        gains.at[core], gains.at[core], pair_send.at[2], pair_recv.at[2],
        device_id={"tile": partner}, device_id_type=MESH,
    )
    send_gain.start()

    def scale_side(side):
        for v in range(nlane):
            gain = jnp.broadcast_to(gains[side, v : v + 1, :], (LANES, LANES)).T
            top = slice(v * LANES, (v + 1) * LANES)
            low = slice(chans + v * LANES, chans + (v + 1) * LANES)
            for q in range(chunks):
                span = slice(q * LANES, (q + 1) * LANES)
                real = (echo[side, 0, top, span].astype(F32) * gain).astype(BF16)
                imag = (echo[side, 1, top, span].astype(F32) * gain).astype(BF16)
                rhs[q, side, top, :LANES] = real
                rhs[q, side, low, :LANES] = -imag
                rhs[q, side, top, LANES:] = imag
                rhs[q, side, low, LANES:] = real

    scale_side(core)
    send_echo.wait_recv()
    send_gain.wait_recv()
    scale_side(1 - core)
    send_perm.wait_recv()

    def partial_beams(q, dest):
        return jnp.dot(perm[0, dest], rhs[q, 0], preferred_element_type=F32) + jnp.dot(
            perm[1, dest], rhs[q, 1], preferred_element_type=F32
        )

    x_copies = []
    for q in range(chunks):
        for s, peer in enumerate(x_peers):
            xsend[q, s] = partial_beams(q, peer // 2).astype(BF16)
            copy = pltpu.make_async_remote_copy(
                xsend.at[q, s], xrecv.at[q, s], x_send.at[q, s], x_recv.at[q, s],
                device_id={"tile": peer}, device_id_type=MESH,
            )
            copy.start()
            x_copies.append(copy)
        own[q] = partial_beams(q, chip_x)

    step = 64
    for q in range(chunks):
        for s in range(3):
            x_copies[3 * q + s].wait_recv()

        @pl.loop(0, slots // step)
        def _(r):
            rows = pl.ds(pl.multiple_of(r * step, step), step)
            both = own[q, rows, :]
            for s in range(3):
                both = both + xrecv[q, s, rows, :].astype(F32)
            tiled = (step // 8, 8, LANES)
            real, imag = both[:, :LANES].reshape(tiled), both[:, LANES:].reshape(tiled)
            cut = limit[rows, :].reshape(tiled)
            out_re = jnp.zeros(tiled, F32)
            out_im = jnp.zeros(tiled, F32)
            for tap in range(TAPS):
                live = cut > float(tap)
                shift_re = real if tap == 0 else pltpu.roll(real, LANES - tap, 2)
                shift_im = imag if tap == 0 else pltpu.roll(imag, LANES - tap, 2)
                shift_re = jnp.where(live, shift_re, 0.0)
                shift_im = jnp.where(live, shift_im, 0.0)
                code_re = coef[2 * tap]
                code_im = coef[2 * tap + 1]
                out_re = out_re + (code_re * shift_re + code_im * shift_im)
                out_im = out_im + (code_re * shift_im - code_im * shift_re)
            kept = pulses[rows, :].reshape(tiled) > float(q * (LANES // G))
            weave[pl.ds(r * (2 * step), step, stride=2), :] = jnp.where(kept, out_re, 0.0).reshape(step, LANES)
            weave[pl.ds(r * (2 * step) + 1, step, stride=2), :] = jnp.where(kept, out_im, 0.0).reshape(step, LANES)

        zsend[q] = weave[...].reshape(zsend.shape[1:]).astype(BF16)

        @pl.loop(0, nb - 1)
        def _(i):
            peer = plane_peer(i)
            pltpu.make_async_remote_copy(
                zsend.at[q, peer], out_ref.at[q, beam], z_send.at[q], z_recv.at[q],
                device_id={"beam": peer}, device_id_type=MESH,
            ).start()

        pltpu.make_async_copy(zsend.at[q, beam], out_ref.at[q, beam], self_sem.at[q]).start()

    for q in range(chunks):
        arrived = out_ref.at[q, pl.ds(0, nb - 1)]
        pltpu.make_async_copy(arrived, arrived, z_recv.at[q]).wait()
        pltpu.make_async_copy(zsend.at[q, beam], out_ref.at[q, beam], self_sem.at[q]).wait()

    pltpu.make_async_copy(everyone, everyone, ar_send).wait()
    send_echo.wait_send()
    send_perm.wait_send()
    send_gain.wait_send()
    for copy in x_copies:
        copy.wait_send()
    for q in range(chunks):
        sent = zsend.at[q, pl.ds(0, nb - 1)]
        pltpu.make_async_copy(sent, sent, z_send.at[q]).wait()


def exchange(nb, echoes, steer, code, beam_order, dwell, code_len):
    chans, columns = echoes.shape[1], echoes.shape[2]
    total = steer.shape[1]
    slots = total // 8
    chunks = columns // LANES
    rows = 2 * slots // nb
    blocks = total // LANES
    vmem = pl.BlockSpec(memory_space=pltpu.VMEM)
    hbm = pl.BlockSpec(memory_space=pltpu.HBM)
    dma = pltpu.SemaphoreType.DMA

    def body(*refs):
        exchange_kernel(nb, *refs)

    return pl.pallas_call(
        body,
        out_shape=jax.ShapeDtypeStruct((chunks, nb, rows, LANES), BF16),
        in_specs=[hbm] * 6,
        out_specs=vmem,
        scratch_shapes=[
            pltpu.VMEM((blocks, LANES), jnp.int32),
            pltpu.VMEM((blocks, LANES), jnp.int32),
            pltpu.VMEM((blocks, LANES), jnp.int32),
            pltpu.VMEM(code.shape, BF16),
            pltpu.VMEM((2 * TAPS, 8, LANES), F32),
            pltpu.VMEM((2, 2, chans, columns), BF16),
            pltpu.VMEM(steer.shape, BF16),
            pltpu.VMEM((blocks, LANES, LANES), F32),
            pltpu.VMEM((2, 4, slots, 2 * chans), BF16),
            pltpu.VMEM((4, slots, 2 * chans), BF16),
            pltpu.VMEM((nb, chans // LANES, LANES), F32),
            pltpu.VMEM((2, chans // LANES, LANES), F32),
            pltpu.VMEM((slots, LANES), F32),
            pltpu.VMEM((slots, LANES), F32),
            pltpu.VMEM((chunks, 2, 2 * chans, 2 * LANES), BF16),
            pltpu.VMEM((chunks, 3, slots, 2 * LANES), BF16),
            pltpu.VMEM((chunks, slots, 2 * LANES), F32),
            pltpu.VMEM((chunks, 3, slots, 2 * LANES), BF16),
            pltpu.VMEM((2 * slots, LANES), F32),
            pltpu.VMEM((chunks, nb, rows, LANES), BF16),
            dma((6,)), dma, dma, dma((3,)), dma((3,)),
            dma((chunks, 3)), dma((chunks, 3)), dma((chunks,)), dma((chunks,)), dma((chunks,)),
        ],
        compiler_params=pltpu.CompilerParams(
            collective_id=0, has_side_effects=True, vmem_limit_bytes=40 << 20
        ),
        name="exchange",
    )(
        *[
            pltpu.with_memory_space_constraint(x, pltpu.HBM)
            for x in (
                echoes, steer,
                beam_order.reshape(blocks, LANES), dwell.reshape(blocks, LANES), code_len.reshape(blocks, LANES),
                code,
            )
        ]
    )


def dft_tables(nb, chunks, pulses_all):
    length = nb * chunks
    radix = pulses_all // length
    index = (np.arange(nb)[None, :] * chunks + np.arange(chunks)[:, None]).reshape(-1)
    angle = -2.0 * np.pi * ((index[:, None] * np.arange(length)[None, :]) % length) / length
    real, imag = np.cos(angle), np.sin(angle)
    table = np.block([[real, imag], [-imag, real]])
    turn = -2.0 * np.pi * np.arange(radix)[:, None] * np.arange(length)[None, :] / pulses_all
    twist = np.concatenate([np.cos(turn), np.sin(turn)], axis=0) / math.sqrt(pulses_all)
    return jnp.asarray(table, BF16), jnp.asarray(twist, F32)


def dft_kernel(x_ref, table_ref, twist_ref, out_ref, wide):
    chunks, nb, rows, _ = x_ref.shape
    length = chunks * nb
    slot = pl.program_id(0)

    @pl.when(slot == 0)
    def _():
        wide[...] = x_ref[...].astype(F32).reshape(wide.shape)

    real = wide[pl.ds(2 * slot, length, stride=rows), :].T.astype(BF16)
    imag = wide[pl.ds(2 * slot + 1, length, stride=rows), :].T.astype(BF16)
    left = jnp.concatenate([real, imag], axis=1)
    found = jnp.dot(left, table_ref[...], preferred_element_type=F32)
    re, im = [], []
    for p in range(4):
        fr = found[p * G : (p + 1) * G, :length]
        fi = found[p * G : (p + 1) * G, length:]
        wr = twist_ref[p : p + 1, :]
        wi = twist_ref[4 + p : 5 + p, :]
        re.append(fr * wr - fi * wi)
        im.append(fr * wi + fi * wr)
    even_re, even_im = re[0] + re[2], im[0] + im[2]
    odd_re, odd_im = re[0] - re[2], im[0] - im[2]
    side_re, side_im = re[1] + re[3], im[1] + im[3]
    turn_re, turn_im = re[1] - re[3], im[1] - im[3]
    parts = [
        (even_re + side_re, even_im + side_im),
        (odd_re + turn_im, odd_im - turn_re),
        (even_re - side_re, even_im - side_im),
        (odd_re - turn_im, odd_im + turn_re),
    ]
    for k, (a, b) in enumerate(parts):
        out_ref[0, 0, :, k * length : (k + 1) * length] = a
        out_ref[0, 1, :, k * length : (k + 1) * length] = b


def doppler(x, pulses_all):
    chunks, nb, rows, _ = x.shape
    table, twist = dft_tables(nb, chunks, pulses_all)
    vmem = pl.BlockSpec(memory_space=pltpu.VMEM)
    return pl.pallas_call(
        dft_kernel,
        grid=(rows // 2,),
        out_shape=jax.ShapeDtypeStruct((rows // 2, 2, G, pulses_all), F32),
        in_specs=[vmem, vmem, vmem],
        out_specs=pl.BlockSpec((1, 2, G, pulses_all), lambda n: (n, 0, 0, 0)),
        scratch_shapes=[pltpu.VMEM((chunks * nb * rows, LANES), F32)],
        compiler_params=pltpu.CompilerParams(vmem_limit_bytes=8 << 20),
        name="doppler",
    )(x, table, twist)


def solution(mesh):
    nb = mesh.shape["beam"]

    def on_device(echoes, steer, code, beam_order, dwell, code_len):
        arrived = exchange(nb, echoes, steer, code, beam_order, dwell, code_len)
        return doppler(arrived, nb * echoes.shape[2] // G)

    placed = (P(None, "tile", "beam"), P(None, None, "tile"), P(), P(), P(), P())
    return jax.shard_map(
        on_device,
        mesh=mesh,
        in_specs=placed,
        out_specs=P(("tile", "beam"), None, None, None),
        check_vma=False,
    )
```

```python
import math

import jax
import jax.numpy as jnp
import numpy as np
from jax import lax
from jax.experimental import pallas as pl
from jax.experimental.pallas import tpu as pltpu
from jax.sharding import PartitionSpec as P

G = 32
TAPS = 8
LANES = 128
MESH = pl.DeviceIdType.MESH
F32 = jnp.float32
BF16 = jnp.bfloat16


def exchange_kernel(
    nb,
    echo_hbm, steer_hbm, order_hbm, dwell_hbm, lens_hbm, code_hbm,
    out_ref,
    order_ref, dwell_ref, lens_ref, code_ref, coef,
    echo, steer, cols, perm, perm_out, power, stage, gathered, gains, spread, limit, pulses, rhs, far_out, far_in, near_out, near_in, hold, own, weave, zsend,
    local_sem, ar_send, ar_recv, pair_send, pair_recv, far_send, far_recv, near_send, near_recv, z_send, z_recv, self_sem,
):
    nz = min(16, nb)
    ny = nb // nz
    tile = lax.axis_index("tile")
    beam = lax.axis_index("beam")
    core = lax.rem(tile, 2)
    chip_x = tile // 2
    my_y = beam // nz
    my_z = lax.rem(beam, nz)
    chans = echo.shape[2]
    chunks = zsend.shape[0]
    slots = perm.shape[2]
    rows_total = steer.shape[1]
    blocks = rows_total // LANES
    half_blocks = slots // LANES
    nlane = chans // LANES

    other = 2 * chip_x + 1 - core
    ys = [lax.rem(my_y + d, ny) for d in range(ny)]

    def zs(d):
        return lax.rem(my_z + (d + nz), nz)

    def at(side, y, z):
        return {"tile": side, "beam": y * nz + z}

    def start_plane_sends(source, target, sent, received):
        def send(y, z):
            peer = y * nz + z
            pltpu.make_async_remote_copy(
                source(peer), target, sent, received, device_id={"beam": peer}, device_id_type=MESH
            ).start()

        for y in ys:
            send(y, zs(nz // 2))

        @pl.loop(1, nz // 2)
        def _(m):
            for z in (zs(nz // 2 + m - nz), zs(nz // 2 - m)):
                for y in ys:
                    send(y, z)

        for y in ys[1:]:
            send(y, my_z)

    get_echo = pltpu.make_async_copy(echo_hbm, echo.at[core], local_sem.at[0])
    get_steer = pltpu.make_async_copy(steer_hbm, steer, local_sem.at[1])
    small = [
        pltpu.make_async_copy(source, target, local_sem.at[2 + n])
        for n, (source, target) in enumerate(
            [(order_hbm, order_ref), (dwell_hbm, dwell_ref), (lens_hbm, lens_ref), (code_hbm, code_ref)]
        )
    ]
    for copy in small[:1]:
        copy.start()
    get_echo.start()
    get_steer.start()
    for copy in small[1:]:
        copy.start()

    barrier = pltpu.get_barrier_semaphore()

    sides = [lax.rem(chip_x + d, 4) for d in (1, 3)]
    greeted = [at(tile, my_y, zs(d)) for d in (-4, -3, -2, -1, 1, 2, 3, 4)]
    greeted += [at(tile, y, zs(d)) for y in ys[1:] for d in (0, 4, -4)]
    greeted += [at(other, y, zs(d)) for y in ys for d in (0, 4, -4)]
    greeted += [{"tile": 2 * side + core} for side in sides]
    for peer in greeted:
        pl.semaphore_signal(barrier, inc=1, device_id=peer, device_id_type=MESH)

    small[0].wait()
    order_cols = order_ref[...].astype(F32)
    lane = lax.broadcasted_iota(jnp.int32, (LANES, LANES), 1)
    for b in range(blocks):
        cols[b] = jnp.broadcast_to(order_cols[b : b + 1, :], (LANES, LANES)).T

    get_echo.wait()
    for v in range(nlane):
        total = jnp.zeros((LANES, LANES), F32)
        for c in range(2):
            for q in range(chunks):
                part = echo[core, c, v * LANES : (v + 1) * LANES, q * LANES : (q + 1) * LANES].astype(F32)
                total = total + part * part
        power[4, v : v + 1, :] = jnp.sum(total.T, axis=0, keepdims=True)

    lane_f = lane.astype(F32)

    def one_hot_block(b):
        col = cols[b]
        return [(col == lane_f + float(w * LANES)) for w in range(blocks)]

    def permuted(b):
        hot = jnp.concatenate([m.astype(F32).astype(BF16) for m in one_hot_block(b)], axis=1)
        left = jnp.dot(hot, steer[0], preferred_element_type=F32)
        right = jnp.dot(hot, steer[1], preferred_element_type=F32)
        return left.astype(BF16), right.astype(BF16)

    get_steer.wait()

    def permute(target, side, first, last):
        @pl.loop(first, last)
        def _(i):
            dest = i // half_blocks
            u = lax.rem(i, half_blocks)
            left, right = permuted((dest * 2 + side) * half_blocks + u)
            rows = pl.ds(pl.multiple_of(u * LANES, LANES), LANES)
            target[dest, rows, :chans] = left
            target[dest, rows, chans:] = right

    permute(perm_out, 1 - core, 0, 2 * half_blocks)
    pl.semaphore_wait(barrier, len(greeted))

    for d in (-4, 4, -3, 3, -2, 2, -1, 1):
        pltpu.make_async_remote_copy(
            power.at[4], power.at[4 - d], ar_send.at[0], ar_recv.at[0],
            device_id=at(tile, my_y, zs(d)), device_id_type=MESH,
        ).start()

    send_echo = pltpu.make_async_remote_copy(
        echo.at[core], echo.at[core], pair_send.at[0], pair_recv.at[0],
        device_id={"tile": other}, device_id_type=MESH,
    )
    send_echo.start()
    permute(perm_out, 1 - core, 2 * half_blocks, 4 * half_blocks)
    send_perm = pltpu.make_async_remote_copy(
        perm_out, perm.at[core], pair_send.at[1], pair_recv.at[1],
        device_id={"tile": other}, device_id_type=MESH,
    )
    send_perm.start()
    permute(perm.at[core], core, 0, 2 * half_blocks)

    nearby = power.at[pl.ds(0, 8)]
    pltpu.make_async_copy(nearby, nearby, ar_recv.at[0]).wait()
    around = jnp.sum(power[...], axis=0)
    stage[0] = around
    stage[1] = jnp.sum(power[5:9], axis=0)
    stage[2] = jnp.sum(power[1:4], axis=0)
    gathered[(core * 3) * ny + my_y] = around
    for kind, d in ((1, -4), (2, 4), (0, 0)):
        for step, y in enumerate(ys):
            for side in (tile, other):
                if kind == 0 and step == 0 and side is tile:
                    continue
                pltpu.make_async_remote_copy(
                    stage.at[kind], gathered.at[(core * 3 + kind) * ny + my_y], ar_send.at[1], ar_recv.at[1],
                    device_id=at(side, y, zs(d)), device_id_type=MESH,
                ).start()
    permute(perm.at[core], core, 2 * half_blocks, 4 * half_blocks)

    for copy in small[1:]:
        copy.wait()
    taps = code_ref[...].astype(F32)
    for tap in range(TAPS):
        for c in range(2):
            coef[2 * tap + c] = jnp.broadcast_to(taps[c : c + 1, tap : tap + 1], coef.shape[1:])

    for u in range(half_blocks):
        masks = one_hot_block(tile * half_blocks + u)
        length = jnp.zeros((LANES, LANES), F32)
        keep = jnp.zeros((LANES, LANES), F32)
        for w in range(blocks):
            length = length + jnp.where(masks[w], lens_ref[w : w + 1, :].astype(F32), 0.0)
            keep = keep + jnp.where(masks[w], dwell_ref[w : w + 1, :].astype(F32), 0.0)
        length = jnp.sum(length, axis=1, keepdims=True)
        keep = jnp.sum(keep, axis=1, keepdims=True)
        gate = lax.rem(lane, G).astype(F32)
        limit[u * LANES : (u + 1) * LANES, :] = jnp.minimum(jnp.broadcast_to(length, (LANES, LANES)), G - gate)
        first = (lane // G + beam * (chunks * (LANES // G))).astype(F32)
        pulses[u * LANES : (u + 1) * LANES, :] = jnp.broadcast_to(keep, (LANES, LANES)) - first

    everyone = gathered.at[pl.ds(0, 6 * ny - 1)]
    pltpu.make_async_copy(everyone, everyone, ar_recv.at[1]).wait()
    for side in range(2):
        total = jnp.sum(gathered[side * 3 * ny : (side + 1) * 3 * ny], axis=0)
        gains[side] = lax.rsqrt(total * (1.0 / (nb * chunks * LANES)) + 1e-05)

    def spread_gain(side):
        for v in range(nlane):
            spread[side, v] = jnp.broadcast_to(gains[side, v : v + 1, :], (LANES, LANES)).T

    def scale(side, q):
        for v in range(nlane):
            gain = spread[side, v]
            top = slice(v * LANES, (v + 1) * LANES)
            low = slice(chans + v * LANES, chans + (v + 1) * LANES)
            span = slice(q * LANES, (q + 1) * LANES)
            real = (echo[side, 0, top, span].astype(F32) * gain).astype(BF16)
            imag = (echo[side, 1, top, span].astype(F32) * gain).astype(BF16)
            rhs[q, side, top, :LANES] = real
            rhs[q, side, low, :LANES] = -imag
            rhs[q, side, top, LANES:] = imag
            rhs[q, side, low, LANES:] = real

    send_echo.wait_recv()
    send_perm.wait_recv()
    spread_gain(0)
    spread_gain(1)

    def partial_beams(q, dest):
        return jnp.dot(perm[0, dest], rhs[q, 0], preferred_element_type=F32) + jnp.dot(
            perm[1, dest], rhs[q, 1], preferred_element_type=F32
        )

    half = slots // 2
    direct = [slice(half, slots), slice(0, half)]
    summed = [slice(0, half), slice(half, slots)]
    x_copies = []

    def to_side(side, source, target, sent, received):
        copy = pltpu.make_async_remote_copy(
            source, target, sent, received,
            device_id={"tile": 2 * sides[side] + core}, device_id_type=MESH,
        )
        copy.start()
        x_copies.append(copy)
        return copy

    far, near = {}, {}

    def form(q):
        scale(0, q)
        scale(1, q)
        product = partial_beams(q, lax.rem(chip_x + 2, 4))
        for side in range(2):
            far_out[q, side] = product[summed[side]].astype(BF16)
        for side in range(2):
            product = partial_beams(q, sides[side])
            near_out[q, side, direct[side]] = product[direct[side]].astype(BF16)
            hold[q, side] = product[summed[side]]
        own[q] = partial_beams(q, chip_x)

    def start_far(q):
        for side in range(2):
            far[q, side] = to_side(
                side, far_out.at[q, side], far_in.at[q, side], far_send.at[q, side], far_recv.at[q, side]
            )

    def start_near(q):
        for side in range(2):
            part = direct[side]
            near[q, side, 0] = to_side(
                side, near_out.at[q, side, part], near_in.at[q, side, part],
                near_send.at[q, side, 0], near_recv.at[q, side, 0],
            )

    def relay(q):
        for side in range(2):
            far[q, side].wait_recv()
            part = summed[side]
            near_out[q, side, part] = (hold[q, side] + far_in[q, side].astype(F32)).astype(BF16)
            near[q, side, 1] = to_side(
                side, near_out.at[q, side, part], near_in.at[q, side, part],
                near_send.at[q, side, 1], near_recv.at[q, side, 1],
            )

    step = 64

    def finish(q):
        for side in range(2):
            for n in range(2):
                near[q, side, n].wait_recv()

        @pl.loop(0, slots // step)
        def _(r):
            rows = pl.ds(pl.multiple_of(r * step, step), step)
            both = own[q, rows, :]
            for side in range(2):
                both = both + near_in[q, side, rows, :].astype(F32)
            tiled = (step // 8, 8, LANES)
            real, imag = both[:, :LANES].reshape(tiled), both[:, LANES:].reshape(tiled)
            cut = limit[rows, :].reshape(tiled)
            out_re = jnp.zeros(tiled, F32)
            out_im = jnp.zeros(tiled, F32)
            for tap in range(TAPS):
                live = cut > float(tap)
                shift_re = real if tap == 0 else pltpu.roll(real, LANES - tap, 2)
                shift_im = imag if tap == 0 else pltpu.roll(imag, LANES - tap, 2)
                shift_re = jnp.where(live, shift_re, 0.0)
                shift_im = jnp.where(live, shift_im, 0.0)
                code_re = coef[2 * tap]
                code_im = coef[2 * tap + 1]
                out_re = out_re + (code_re * shift_re + code_im * shift_im)
                out_im = out_im + (code_re * shift_im - code_im * shift_re)
            kept = pulses[rows, :].reshape(tiled) > float(q * (LANES // G))
            weave[pl.ds(r * (2 * step), step, stride=2), :] = jnp.where(kept, out_re, 0.0).reshape(step, LANES)
            weave[pl.ds(r * (2 * step) + 1, step, stride=2), :] = jnp.where(kept, out_im, 0.0).reshape(step, LANES)

        zsend[q] = weave[...].reshape(zsend.shape[1:]).astype(BF16)

        start_plane_sends(lambda peer: zsend.at[q, peer], out_ref.at[q, beam], z_send.at[q], z_recv.at[q])
        pltpu.make_async_copy(zsend.at[q, beam], out_ref.at[q, beam], self_sem.at[q]).start()

    form(0)
    start_far(0)
    start_near(0)
    form(1)
    for q in range(chunks):
        relay(q)
        if q + 1 < chunks:
            start_far(q + 1)
            start_near(q + 1)
        if q + 2 < chunks:
            form(q + 2)
        finish(q)

    for q in range(chunks):
        arrived = out_ref.at[q, pl.ds(0, nb - 1)]
        pltpu.make_async_copy(arrived, arrived, z_recv.at[q]).wait()
        pltpu.make_async_copy(zsend.at[q, beam], out_ref.at[q, beam], self_sem.at[q]).wait()

    pltpu.make_async_copy(nearby, nearby, ar_send.at[0]).wait()
    pltpu.make_async_copy(everyone, everyone, ar_send.at[1]).wait()
    send_echo.wait_send()
    send_perm.wait_send()
    for copy in x_copies:
        copy.wait_send()
    for q in range(chunks):
        sent = zsend.at[q, pl.ds(0, nb - 1)]
        pltpu.make_async_copy(sent, sent, z_send.at[q]).wait()


def exchange(nb, echoes, steer, code, beam_order, dwell, code_len):
    chans, columns = echoes.shape[1], echoes.shape[2]
    total = steer.shape[1]
    slots = total // 8
    chunks = columns // LANES
    rows = 2 * slots // nb
    blocks = total // LANES
    vmem = pl.BlockSpec(memory_space=pltpu.VMEM)
    hbm = pl.BlockSpec(memory_space=pltpu.HBM)
    dma = pltpu.SemaphoreType.DMA

    def body(*refs):
        exchange_kernel(nb, *refs)

    return pl.pallas_call(
        body,
        out_shape=jax.ShapeDtypeStruct((chunks, nb, rows, LANES), BF16),
        in_specs=[hbm] * 6,
        out_specs=vmem,
        scratch_shapes=[
            pltpu.VMEM((blocks, LANES), jnp.int32),
            pltpu.VMEM((blocks, LANES), jnp.int32),
            pltpu.VMEM((blocks, LANES), jnp.int32),
            pltpu.VMEM(code.shape, BF16),
            pltpu.VMEM((2 * TAPS, 8, LANES), F32),
            pltpu.VMEM((2, 2, chans, columns), BF16),
            pltpu.VMEM(steer.shape, BF16),
            pltpu.VMEM((blocks, LANES, LANES), F32),
            pltpu.VMEM((2, 4, slots, 2 * chans), BF16),
            pltpu.VMEM((4, slots, 2 * chans), BF16),
            pltpu.VMEM((9, chans // LANES, LANES), F32),
            pltpu.VMEM((3, chans // LANES, LANES), F32),
            pltpu.VMEM((24, chans // LANES, LANES), F32),
            pltpu.VMEM((2, chans // LANES, LANES), F32),
            pltpu.VMEM((2, chans // LANES, LANES, LANES), F32),
            pltpu.VMEM((slots, LANES), F32),
            pltpu.VMEM((slots, LANES), F32),
            pltpu.VMEM((chunks, 2, 2 * chans, 2 * LANES), BF16),
            pltpu.VMEM((chunks, 2, slots // 2, 2 * LANES), BF16),
            pltpu.VMEM((chunks, 2, slots // 2, 2 * LANES), BF16),
            pltpu.VMEM((chunks, 2, slots, 2 * LANES), BF16),
            pltpu.VMEM((chunks, 2, slots, 2 * LANES), BF16),
            pltpu.VMEM((chunks, 2, slots // 2, 2 * LANES), F32),
            pltpu.VMEM((chunks, slots, 2 * LANES), F32),
            pltpu.VMEM((2 * slots, LANES), F32),
            pltpu.VMEM((chunks, nb, rows, LANES), BF16),
            dma((6,)), dma((2,)), dma((2,)), dma((2,)), dma((2,)),
            dma((chunks, 2)), dma((chunks, 2)), dma((chunks, 2, 2)), dma((chunks, 2, 2)), dma((chunks,)), dma((chunks,)), dma((chunks,)),
        ],
        compiler_params=pltpu.CompilerParams(
            collective_id=0, has_side_effects=True, vmem_limit_bytes=40 << 20
        ),
        name="exchange",
    )(
        *[
            pltpu.with_memory_space_constraint(x, pltpu.HBM)
            for x in (
                echoes, steer,
                beam_order.reshape(blocks, LANES), dwell.reshape(blocks, LANES), code_len.reshape(blocks, LANES),
                code,
            )
        ]
    )


def dft_tables(nb, chunks, pulses_all):
    length = nb * chunks
    radix = pulses_all // length
    index = (np.arange(nb)[None, :] * chunks + np.arange(chunks)[:, None]).reshape(-1)
    angle = -2.0 * np.pi * ((index[:, None] * np.arange(length)[None, :]) % length) / length
    real, imag = np.cos(angle), np.sin(angle)
    table = np.block([[real, imag], [-imag, real]])
    turn = -2.0 * np.pi * np.arange(radix)[:, None] * np.arange(length)[None, :] / pulses_all
    twist = np.concatenate([np.cos(turn), np.sin(turn)], axis=0) / math.sqrt(pulses_all)
    return jnp.asarray(table, BF16), jnp.asarray(twist, F32)


def dft_kernel(x_ref, table_ref, twist_ref, out_ref, wide):
    chunks, nb, rows, _ = x_ref.shape
    length = chunks * nb
    slot = pl.program_id(0)

    @pl.when(slot == 0)
    def _():
        wide[...] = x_ref[...].astype(F32).reshape(wide.shape)

    real = wide[pl.ds(2 * slot, length, stride=rows), :].T.astype(BF16)
    imag = wide[pl.ds(2 * slot + 1, length, stride=rows), :].T.astype(BF16)
    left = jnp.concatenate([real, imag], axis=1)
    found = jnp.dot(left, table_ref[...], preferred_element_type=F32)
    re, im = [], []
    for p in range(4):
        fr = found[p * G : (p + 1) * G, :length]
        fi = found[p * G : (p + 1) * G, length:]
        wr = twist_ref[p : p + 1, :]
        wi = twist_ref[4 + p : 5 + p, :]
        re.append(fr * wr - fi * wi)
        im.append(fr * wi + fi * wr)
    even_re, even_im = re[0] + re[2], im[0] + im[2]
    odd_re, odd_im = re[0] - re[2], im[0] - im[2]
    side_re, side_im = re[1] + re[3], im[1] + im[3]
    turn_re, turn_im = re[1] - re[3], im[1] - im[3]
    parts = [
        (even_re + side_re, even_im + side_im),
        (odd_re + turn_im, odd_im - turn_re),
        (even_re - side_re, even_im - side_im),
        (odd_re - turn_im, odd_im + turn_re),
    ]
    for k, (a, b) in enumerate(parts):
        out_ref[0, 0, :, k * length : (k + 1) * length] = a
        out_ref[0, 1, :, k * length : (k + 1) * length] = b


def doppler(x, pulses_all):
    chunks, nb, rows, _ = x.shape
    table, twist = dft_tables(nb, chunks, pulses_all)
    vmem = pl.BlockSpec(memory_space=pltpu.VMEM)
    return pl.pallas_call(
        dft_kernel,
        grid=(rows // 2,),
        out_shape=jax.ShapeDtypeStruct((rows // 2, 2, G, pulses_all), F32),
        in_specs=[vmem, vmem, vmem],
        out_specs=pl.BlockSpec((1, 2, G, pulses_all), lambda n: (n, 0, 0, 0)),
        scratch_shapes=[pltpu.VMEM((chunks * nb * rows, LANES), F32)],
        compiler_params=pltpu.CompilerParams(vmem_limit_bytes=8 << 20),
        name="doppler",
    )(x, table, twist)


def solution(mesh):
    nb = mesh.shape["beam"]

    def on_device(echoes, steer, code, beam_order, dwell, code_len):
        arrived = exchange(nb, echoes, steer, code, beam_order, dwell, code_len)
        return doppler(arrived, nb * echoes.shape[2] // G)

    placed = (P(None, "tile", "beam"), P(None, None, "tile"), P(), P(), P(), P())
    return jax.shard_map(
        on_device,
        mesh=mesh,
        in_specs=placed,
        out_specs=P(("tile", "beam"), None, None, None),
        check_vma=False,
    )
```

```python
import math

import jax
import jax.numpy as jnp
import numpy as np
from jax import lax
from jax.experimental import pallas as pl
from jax.experimental.pallas import tpu as pltpu
from jax.sharding import PartitionSpec as P

G = 32
TAPS = 8
LANES = 128
MESH = pl.DeviceIdType.MESH
F32 = jnp.float32
BF16 = jnp.bfloat16


def exchange_kernel(
    nb,
    echo_hbm, steer_hbm, order_hbm, dwell_hbm, lens_hbm, code_hbm,
    out_ref,
    order_ref, dwell_ref, lens_ref, code_ref, coef,
    echo, steer, cols, perm, perm_out, power, stage, gathered, gains, spread, limit, pulses, rhs, far_out, far_in, near_out, near_in, hold, own, weave, zsend, zrecv, wide,
    local_sem, ar_send, ar_recv, pair_send, pair_recv, far_send, far_recv, near_send, near_recv, z_send, z_recv, self_sem,
):
    nz = min(16, nb)
    ny = nb // nz
    tile = lax.axis_index("tile")
    beam = lax.axis_index("beam")
    core = lax.rem(tile, 2)
    chip_x = tile // 2
    my_y = beam // nz
    my_z = lax.rem(beam, nz)
    chans = echo.shape[2]
    chunks = zsend.shape[0]
    slots = perm.shape[2]
    rows_total = steer.shape[1]
    blocks = rows_total // LANES
    half_blocks = slots // LANES
    nlane = chans // LANES

    other = 2 * chip_x + 1 - core
    ys = [lax.rem(my_y + d, ny) for d in range(ny)]

    def zs(d):
        return lax.rem(my_z + (d + nz), nz)

    def at(side, y, z):
        return {"tile": side, "beam": y * nz + z}

    def start_plane_sends(q, steps):
        def send(k, z):
            pltpu.make_async_remote_copy(
                zsend.at[q, k, z], zrecv.at[q, beam], z_send.at[q], z_recv.at[q],
                device_id={"beam": ys[k] * nz + z}, device_id_type=MESH,
            ).start()

        for k in steps:
            send(k, zs(nz // 2))

        @pl.loop(1, nz // 2)
        def _(m):
            for z in (zs(m - nz // 2), zs(nz // 2 - m)):
                for k in steps:
                    send(k, z)

        for k in steps:
            if k > 0:
                send(k, my_z)

    get_echo = pltpu.make_async_copy(echo_hbm, echo.at[core], local_sem.at[0])
    get_steer = pltpu.make_async_copy(steer_hbm, steer, local_sem.at[1])
    small = [
        pltpu.make_async_copy(source, target, local_sem.at[2 + n])
        for n, (source, target) in enumerate(
            [(order_hbm, order_ref), (dwell_hbm, dwell_ref), (lens_hbm, lens_ref), (code_hbm, code_ref)]
        )
    ]
    for copy in small[:1]:
        copy.start()
    get_echo.start()
    get_steer.start()
    for copy in small[1:]:
        copy.start()

    barrier = pltpu.get_barrier_semaphore()

    sides = [lax.rem(chip_x + d, 4) for d in (1, 3)]
    greeted = [at(tile, my_y, zs(d)) for d in (-4, -3, -2, -1, 1, 2, 3, 4)]
    greeted += [at(tile, y, my_z) for y in ys[1:]]
    greeted += [at(other, y, my_z) for y in ys]
    across = lax.rem(chip_x + 2, 4)
    greeted += [{"tile": 2 * side + core} for side in sides + [across]]
    for peer in greeted:
        pl.semaphore_signal(barrier, inc=1, device_id=peer, device_id_type=MESH)

    lane = lax.broadcasted_iota(jnp.int32, (LANES, LANES), 1)
    get_echo.wait()
    for v in range(nlane):
        total = jnp.zeros((LANES, LANES), F32)
        for c in range(2):
            for q in range(chunks):
                part = echo[core, c, v * LANES : (v + 1) * LANES, q * LANES : (q + 1) * LANES].astype(F32)
                total = total + part * part
        power[4, v : v + 1, :] = jnp.sum(total.T, axis=0, keepdims=True)

    lane_f = lane.astype(F32)

    def one_hot_block(b):
        col = cols[b]
        return [(col == lane_f + float(w * LANES)) for w in range(blocks)]

    def permuted(b):
        hot = jnp.concatenate([m.astype(F32).astype(BF16) for m in one_hot_block(b)], axis=1)
        left = jnp.dot(hot, steer[0], preferred_element_type=F32)
        right = jnp.dot(hot, steer[1], preferred_element_type=F32)
        return left.astype(BF16), right.astype(BF16)

    def permute(target, side, first, last):
        @pl.loop(first, last)
        def _(i):
            dest = i // half_blocks
            u = lax.rem(i, half_blocks)
            left, right = permuted((dest * 2 + side) * half_blocks + u)
            rows = pl.ds(pl.multiple_of(u * LANES, LANES), LANES)
            target[dest, rows, :chans] = left
            target[dest, rows, chans:] = right

    small[0].wait()
    order_cols = order_ref[...].astype(F32)
    for b in range(blocks):
        cols[b] = jnp.broadcast_to(order_cols[b : b + 1, :], (LANES, LANES)).T
    get_steer.wait()
    permute(perm_out, 1 - core, 0, half_blocks)
    pl.semaphore_wait(barrier, len(greeted))

    for d in (-4, 4, -3, 3, -2, 2, -1, 1):
        pltpu.make_async_remote_copy(
            power.at[4], power.at[4 - d], ar_send.at[0], ar_recv.at[0],
            device_id=at(tile, my_y, zs(d)), device_id_type=MESH,
        ).start()

    send_echo = pltpu.make_async_remote_copy(
        echo.at[core], echo.at[core], pair_send.at[0], pair_recv.at[0],
        device_id={"tile": other}, device_id_type=MESH,
    )
    send_echo.start()
    permute(perm_out, 1 - core, half_blocks, 4 * half_blocks)
    send_perm = pltpu.make_async_remote_copy(
        perm_out, perm.at[core], pair_send.at[1], pair_recv.at[1],
        device_id={"tile": other}, device_id_type=MESH,
    )
    send_perm.start()
    nearby = power.at[pl.ds(0, 8)]
    pltpu.make_async_copy(nearby, nearby, ar_recv.at[0]).wait()
    around = jnp.sum(power[...], axis=0)
    stage[0] = around
    stage[1] = jnp.sum(power[5:9], axis=0)
    stage[2] = jnp.sum(power[1:4], axis=0)
    gathered[(core * 3) * ny + my_y] = around
    for kind, d in ((1, -4), (2, 4), (0, 0)):
        for step, y in enumerate(ys):
            for side in (tile, other):
                if kind == 0 and step == 0 and side is tile:
                    continue
                pltpu.make_async_remote_copy(
                    stage.at[kind], gathered.at[(core * 3 + kind) * ny + my_y], ar_send.at[1], ar_recv.at[1],
                    device_id=at(side, y, zs(d)), device_id_type=MESH,
                ).start()
    permute(perm.at[core], core, 0, 4 * half_blocks)

    for copy in small[1:]:
        copy.wait()
    taps = code_ref[...].astype(F32)
    for tap in range(TAPS):
        for c in range(2):
            coef[2 * tap + c] = jnp.broadcast_to(taps[c : c + 1, tap : tap + 1], coef.shape[1:])

    for u in range(half_blocks):
        masks = one_hot_block(tile * half_blocks + u)
        length = jnp.zeros((LANES, LANES), F32)
        keep = jnp.zeros((LANES, LANES), F32)
        for w in range(blocks):
            length = length + jnp.where(masks[w], lens_ref[w : w + 1, :].astype(F32), 0.0)
            keep = keep + jnp.where(masks[w], dwell_ref[w : w + 1, :].astype(F32), 0.0)
        length = jnp.sum(length, axis=1, keepdims=True)
        keep = jnp.sum(keep, axis=1, keepdims=True)
        gate = lax.rem(lane, G).astype(F32)
        limit[u * LANES : (u + 1) * LANES, :] = jnp.minimum(jnp.broadcast_to(length, (LANES, LANES)), G - gate)
        first = (lane // G + beam * (chunks * (LANES // G))).astype(F32)
        pulses[u * LANES : (u + 1) * LANES, :] = jnp.broadcast_to(keep, (LANES, LANES)) - first

    everyone = gathered.at[pl.ds(0, 6 * ny - 1)]
    pltpu.make_async_copy(everyone, everyone, ar_recv.at[1]).wait()
    for side in range(2):
        total = jnp.sum(gathered[side * 3 * ny : (side + 1) * 3 * ny], axis=0)
        gains[side] = lax.rsqrt(total * (1.0 / (nb * chunks * LANES)) + 1e-05)

    def spread_gain(side):
        for v in range(nlane):
            spread[side, v] = jnp.broadcast_to(gains[side, v : v + 1, :], (LANES, LANES)).T

    def scale(side, q):
        for v in range(nlane):
            gain = spread[side, v]
            top = slice(v * LANES, (v + 1) * LANES)
            low = slice(chans + v * LANES, chans + (v + 1) * LANES)
            span = slice(q * LANES, (q + 1) * LANES)
            real = (echo[side, 0, top, span].astype(F32) * gain).astype(BF16)
            imag = (echo[side, 1, top, span].astype(F32) * gain).astype(BF16)
            rhs[q, side, top, :LANES] = real
            rhs[q, side, low, :LANES] = -imag
            rhs[q, side, top, LANES:] = imag
            rhs[q, side, low, LANES:] = real

    send_echo.wait_recv()
    send_perm.wait_recv()
    spread_gain(0)
    spread_gain(1)

    def partial_beams(q, dest):
        return jnp.dot(perm[0, dest], rhs[q, 0], preferred_element_type=F32) + jnp.dot(
            perm[1, dest], rhs[q, 1], preferred_element_type=F32
        )

    units = [(0, (k,)) for k in range(ny)] + [(q, tuple(range(ny))) for q in range(1, chunks)]
    places = [lax.rem(y + ny - my_y, ny) for y in range(ny)]
    block = (ny, 2, slots // (2 * ny), 2 * LANES)
    x_copies = []

    def to_chip(chip, source, target, sent, received):
        copy = pltpu.make_async_remote_copy(
            source, target, sent, received, device_id={"tile": 2 * chip + core}, device_id_type=MESH
        )
        copy.start()
        x_copies.append(copy)
        return copy

    far, near = {}, {}

    def start_far(n):
        q, steps = units[n]
        span = pl.ds(steps[0], len(steps))
        for side in range(2):
            far[n, side] = to_chip(
                across if n == 0 else sides[side], far_out.at[q, side, span], far_in.at[q, side, span],
                far_send.at[n, side], far_recv.at[n, side],
            )

    def start_near(n, side, part, which):
        q, steps = units[n]
        span = pl.ds(steps[0], len(steps))
        near[n, side, which] = to_chip(
            sides[side], near_out.at[q, side, part, span], near_in.at[q, side, part, span],
            near_send.at[n, side, which], near_recv.at[n, side, which],
        )

    def form_far(q):
        product = partial_beams(q, across).reshape(block)
        for y in range(ny):
            for side in range(2):
                far_out[q, side, places[y]] = product[y, side].astype(BF16)

    def form_near(q, side):
        product = partial_beams(q, sides[side]).reshape(block)
        for y in range(ny):
            near_out[q, side, 1 - side, places[y]] = product[y, 1 - side].astype(BF16)
            hold[q, side, places[y]] = product[y, side]
            if q == 0:
                near_out[q, side, side, places[y]] = product[y, side].astype(BF16)

    def form_own(q):
        product = partial_beams(q, chip_x).reshape(block)
        for y in range(ny):
            own[q, places[y]] = product[y].reshape(slots // ny, 2 * LANES)

    def relay(n):
        q, steps = units[n]
        for side in range(2):
            far[n, side].wait_recv()
            for k in steps:
                near_out[q, side, side, k] = (hold[q, side, k] + far_in[q, side, k].astype(F32)).astype(BF16)
            start_near(n, side, side, 1)

    step = slots // ny

    def finish(n):
        q, steps = units[n]
        for side in range(2):
            for which in range(2):
                near[n, side, which].wait_recv()
            if n == 0:
                far[n, side].wait_recv()

        def block_of(k, y):
            rows = pl.ds(pl.multiple_of(y * step, step), step)
            both = own[q, k]
            for side in range(2):
                both = both + jnp.concatenate(
                    [near_in[q, side, part, k].astype(F32) for part in range(2)], axis=0
                )
            if n == 0:
                both = both + jnp.concatenate([far_in[q, part, k].astype(F32) for part in range(2)], axis=0)
            tiled = (step // 8, 8, LANES)
            real, imag = both[:, :LANES].reshape(tiled), both[:, LANES:].reshape(tiled)
            cut = limit[rows, :].reshape(tiled)
            out_re = jnp.zeros(tiled, F32)
            out_im = jnp.zeros(tiled, F32)
            for tap in range(TAPS):
                live = cut > float(tap)
                shift_re = real if tap == 0 else pltpu.roll(real, LANES - tap, 2)
                shift_im = imag if tap == 0 else pltpu.roll(imag, LANES - tap, 2)
                shift_re = jnp.where(live, shift_re, 0.0)
                shift_im = jnp.where(live, shift_im, 0.0)
                code_re = coef[2 * tap]
                code_im = coef[2 * tap + 1]
                out_re = out_re + (code_re * shift_re + code_im * shift_im)
                out_im = out_im + (code_re * shift_im - code_im * shift_re)
            kept = pulses[rows, :].reshape(tiled) > float(q * (LANES // G))
            weave[k, pl.ds(0, step, stride=2), :] = jnp.where(kept, out_re, 0.0).reshape(step, LANES)
            weave[k, pl.ds(1, step, stride=2), :] = jnp.where(kept, out_im, 0.0).reshape(step, LANES)
            zsend[q, k] = weave[k].reshape(zsend.shape[2:]).astype(BF16)

        if len(steps) == 1:
            block_of(steps[0], ys[steps[0]])
        else:

            @pl.loop(0, ny)
            def _(k):
                block_of(k, lax.rem(my_y + k, ny))

        start_plane_sends(q, steps)
        if 0 in steps:
            pltpu.make_async_copy(zsend.at[q, 0, my_z], zrecv.at[q, beam], self_sem.at[q]).start()

    scale(0, 0)
    scale(1, 0)
    form_far(0)
    for n in range(ny):
        start_far(n)
    for side in range(2):
        form_near(0, side)
        start_near(0, side, 1 - side, 0)
        start_near(0, side, side, 1)
    for side in range(2):
        for n in range(1, ny):
            start_near(n, side, 1 - side, 0)
    def form_rest(q):
        scale(0, q)
        scale(1, q)
        form_far(q)
        form_near(q, 0)
        form_near(q, 1)
        form_own(q)

    def start_rest(n):
        start_far(n)
        for side in range(2):
            start_near(n, side, 1 - side, 0)

    form_own(0)
    form_rest(1)
    form_rest(2)
    form_rest(3)
    for n in range(1, ny):
        relay(n)
    start_rest(ny)
    for n in range(ny):
        finish(n)
    for n in range(ny, len(units)):
        relay(n)
        if n + 1 < len(units):
            start_rest(n + 1)
        finish(n)

    for q in range(chunks):
        arrived = zrecv.at[q, pl.ds(0, nb - 1)]
        pltpu.make_async_copy(arrived, arrived, z_recv.at[q]).wait()
        pltpu.make_async_copy(zsend.at[q, 0, my_z], zrecv.at[q, beam], self_sem.at[q]).wait()
        wide[...] = zrecv[q].astype(F32).reshape(wide.shape)
        for slot in range(4):
            pair = [wide[pl.ds(2 * slot + c, nb, stride=8), :] for c in range(2)]
            out_ref[slot, :, q * LANES : (q + 1) * LANES] = jnp.concatenate(pair, axis=0).T.astype(BF16)

    pltpu.make_async_copy(nearby, nearby, ar_send.at[0]).wait()
    pltpu.make_async_copy(everyone, everyone, ar_send.at[1]).wait()
    send_echo.wait_send()
    send_perm.wait_send()
    for copy in x_copies:
        copy.wait_send()
    for q in range(chunks):
        sent = zrecv.at[q, pl.ds(0, nb - 1)]
        pltpu.make_async_copy(sent, sent, z_send.at[q]).wait()


def exchange(nb, echoes, steer, code, beam_order, dwell, code_len):
    chans, columns = echoes.shape[1], echoes.shape[2]
    total = steer.shape[1]
    slots = total // 8
    chunks = columns // LANES
    units = chunks + 3
    blocks = total // LANES
    vmem = pl.BlockSpec(memory_space=pltpu.VMEM)
    hbm = pl.BlockSpec(memory_space=pltpu.HBM)
    dma = pltpu.SemaphoreType.DMA

    def body(*refs):
        exchange_kernel(nb, *refs)

    return pl.pallas_call(
        body,
        out_shape=jax.ShapeDtypeStruct((slots // nb, LANES, 2 * nb * chunks), BF16),
        in_specs=[hbm] * 6,
        out_specs=vmem,
        scratch_shapes=[
            pltpu.VMEM((blocks, LANES), jnp.int32),
            pltpu.VMEM((blocks, LANES), jnp.int32),
            pltpu.VMEM((blocks, LANES), jnp.int32),
            pltpu.VMEM(code.shape, BF16),
            pltpu.VMEM((2 * TAPS, 8, LANES), F32),
            pltpu.VMEM((2, 2, chans, columns), BF16),
            pltpu.VMEM(steer.shape, BF16),
            pltpu.VMEM((blocks, LANES, LANES), F32),
            pltpu.VMEM((2, 4, slots, 2 * chans), BF16),
            pltpu.VMEM((4, slots, 2 * chans), BF16),
            pltpu.VMEM((9, chans // LANES, LANES), F32),
            pltpu.VMEM((3, chans // LANES, LANES), F32),
            pltpu.VMEM((24, chans // LANES, LANES), F32),
            pltpu.VMEM((2, chans // LANES, LANES), F32),
            pltpu.VMEM((2, chans // LANES, LANES, LANES), F32),
            pltpu.VMEM((slots, LANES), F32),
            pltpu.VMEM((slots, LANES), F32),
            pltpu.VMEM((chunks, 2, 2 * chans, 2 * LANES), BF16),
            pltpu.VMEM((chunks, 2, 4, slots // 8, 2 * LANES), BF16),
            pltpu.VMEM((chunks, 2, 4, slots // 8, 2 * LANES), BF16),
            pltpu.VMEM((chunks, 2, 2, 4, slots // 8, 2 * LANES), BF16),
            pltpu.VMEM((chunks, 2, 2, 4, slots // 8, 2 * LANES), BF16),
            pltpu.VMEM((chunks, 2, 4, slots // 8, 2 * LANES), F32),
            pltpu.VMEM((chunks, 4, slots // 4, 2 * LANES), F32),
            pltpu.VMEM((4, slots // 2, LANES), F32),
            pltpu.VMEM((chunks, 4, nb // 4, 8, LANES), BF16),
            pltpu.VMEM((chunks, nb, 8, LANES), BF16),
            pltpu.VMEM((nb * 8, LANES), F32),
            dma((6,)), dma((2,)), dma((2,)), dma((2,)), dma((2,)),
            dma((units, 2)), dma((units, 2)), dma((units, 2, 2)), dma((units, 2, 2)), dma((chunks,)), dma((chunks,)), dma((chunks,)),
        ],
        compiler_params=pltpu.CompilerParams(
            collective_id=0, has_side_effects=True, vmem_limit_bytes=40 << 20
        ),
        name="exchange",
    )(
        *[
            pltpu.with_memory_space_constraint(x, pltpu.HBM)
            for x in (
                echoes, steer,
                beam_order.reshape(blocks, LANES), dwell.reshape(blocks, LANES), code_len.reshape(blocks, LANES),
                code,
            )
        ]
    )


def dft_tables(nb, chunks, pulses_all):
    length = nb * chunks
    radix = pulses_all // length
    index = np.arange(nb)[None, :] * chunks + np.arange(chunks)[:, None]
    angle = -2.0 * np.pi * ((index[:, :, None] * np.arange(length)) % length) / length
    real, imag = np.cos(angle), np.sin(angle)
    table = np.concatenate(
        [np.concatenate([real, imag], axis=2), np.concatenate([-imag, real], axis=2)], axis=1
    ).reshape(2 * length, 2 * length)
    turn = -2.0 * np.pi * np.arange(radix)[:, None] * np.arange(length)[None, :] / pulses_all
    twist = np.concatenate([np.cos(turn), np.sin(turn)], axis=0) / math.sqrt(pulses_all)
    return jnp.asarray(table, BF16), jnp.asarray(twist, F32)


def dft_kernel(x_ref, table_ref, twist_ref, out_ref):
    length = x_ref.shape[2] // 2
    found = jnp.dot(x_ref[pl.program_id(0)], table_ref[...], preferred_element_type=F32)
    re, im = [], []
    for p in range(4):
        fr = found[p * G : (p + 1) * G, :length]
        fi = found[p * G : (p + 1) * G, length:]
        wr = twist_ref[p : p + 1, :]
        wi = twist_ref[4 + p : 5 + p, :]
        re.append(fr * wr - fi * wi)
        im.append(fr * wi + fi * wr)
    even_re, even_im = re[0] + re[2], im[0] + im[2]
    odd_re, odd_im = re[0] - re[2], im[0] - im[2]
    side_re, side_im = re[1] + re[3], im[1] + im[3]
    turn_re, turn_im = re[1] - re[3], im[1] - im[3]
    parts = [
        (even_re + side_re, even_im + side_im),
        (odd_re + turn_im, odd_im - turn_re),
        (even_re - side_re, even_im - side_im),
        (odd_re - turn_im, odd_im + turn_re),
    ]
    for k, (a, b) in enumerate(parts):
        out_ref[0, 0, :, k * length : (k + 1) * length] = a
        out_ref[0, 1, :, k * length : (k + 1) * length] = b


def doppler(x, nb, pulses_all):
    slots, _, width = x.shape
    table, twist = dft_tables(nb, width // (2 * nb), pulses_all)
    vmem = pl.BlockSpec(memory_space=pltpu.VMEM)
    return pl.pallas_call(
        dft_kernel,
        grid=(slots,),
        out_shape=jax.ShapeDtypeStruct((slots, 2, G, pulses_all), F32),
        in_specs=[vmem, vmem, vmem],
        out_specs=pl.BlockSpec((1, 2, G, pulses_all), lambda n: (n, 0, 0, 0)),
        compiler_params=pltpu.CompilerParams(vmem_limit_bytes=8 << 20),
        name="doppler",
    )(x, table, twist)


def solution(mesh):
    nb = mesh.shape["beam"]

    def on_device(echoes, steer, code, beam_order, dwell, code_len):
        arrived = exchange(nb, echoes, steer, code, beam_order, dwell, code_len)
        return doppler(arrived, nb, nb * echoes.shape[2] // G)

    placed = (P(None, "tile", "beam"), P(None, None, "tile"), P(), P(), P(), P())
    return jax.shard_map(
        on_device,
        mesh=mesh,
        in_specs=placed,
        out_specs=P(("tile", "beam"), None, None, None),
        check_vma=False,
    )
```

```python
import math

import jax
import jax.numpy as jnp
import numpy as np
from jax import lax
from jax.experimental import pallas as pl
from jax.experimental.pallas import tpu as pltpu
from jax.sharding import PartitionSpec as P

G = 32
TAPS = 8
LANES = 128
MESH = pl.DeviceIdType.MESH
F32 = jnp.float32
BF16 = jnp.bfloat16


def exchange_kernel(
    nb,
    echo_hbm, steer_hbm, order_hbm, dwell_hbm, lens_hbm, code_hbm,
    out_ref,
    order_ref, dwell_ref, lens_ref, code_ref, coef,
    echo, steer, cols, perm, perm_out, power, stage, gathered, gains, spread, limit, pulses, rhs, far_out, far_in, near_out, near_in, hold, own, weave, zsend, zrecv, wide,
    local_sem, ar_send, ar_recv, pair_send, pair_recv, far_send, far_recv, near_send, near_recv, z_send, z_recv, self_sem,
):
    nz = min(16, nb)
    ny = nb // nz
    tile = lax.axis_index("tile")
    beam = lax.axis_index("beam")
    core = lax.rem(tile, 2)
    chip_x = tile // 2
    my_y = beam // nz
    my_z = lax.rem(beam, nz)
    chans = echo.shape[2]
    chunks = zsend.shape[0]
    slots = perm.shape[2]
    rows_total = steer.shape[1]
    blocks = rows_total // LANES
    half_blocks = slots // LANES
    nlane = chans // LANES

    other = 2 * chip_x + 1 - core
    ys = [lax.rem(my_y + d, ny) for d in range(ny)]

    def zs(d):
        return lax.rem(my_z + (d + nz), nz)

    def at(side, y, z):
        return {"tile": side, "beam": y * nz + z}

    def start_plane_sends(q, steps):
        def send(k, z):
            pltpu.make_async_remote_copy(
                zsend.at[q, k, z], zrecv.at[q, beam], z_send.at[q], z_recv.at[q],
                device_id={"beam": ys[k] * nz + z}, device_id_type=MESH,
            ).start()

        if q == chunks - 1:

            @pl.loop(0, nz)
            def _(z):
                for k in steps[1:]:
                    send(k, z)

                @pl.when(z != my_z)
                def _():
                    send(0, z)

            return

        for k in steps:
            send(k, zs(nz // 2))

        @pl.loop(1, nz // 2)
        def _(m):
            for z in (zs(m - nz // 2), zs(nz // 2 - m)):
                for k in steps:
                    send(k, z)

        for k in steps:
            if k > 0:
                send(k, my_z)

    get_echo = pltpu.make_async_copy(echo_hbm, echo.at[core], local_sem.at[0])
    get_steer = pltpu.make_async_copy(steer_hbm, steer, local_sem.at[1])
    small = [
        pltpu.make_async_copy(source, target, local_sem.at[2 + n])
        for n, (source, target) in enumerate(
            [(order_hbm, order_ref), (dwell_hbm, dwell_ref), (lens_hbm, lens_ref), (code_hbm, code_ref)]
        )
    ]
    for copy in small[:1]:
        copy.start()
    get_echo.start()
    get_steer.start()
    for copy in small[1:]:
        copy.start()

    barrier = pltpu.get_barrier_semaphore()

    sides = [lax.rem(chip_x + d, 4) for d in (1, 3)]
    greeted = [at(tile, my_y, zs(d)) for d in (-4, -3, -2, -1, 1, 2, 3, 4)]
    greeted += [at(tile, y, my_z) for y in ys[1:]]
    greeted += [at(other, y, my_z) for y in ys]
    across = lax.rem(chip_x + 2, 4)
    greeted += [{"tile": 2 * side + core} for side in sides + [across]]
    for peer in greeted:
        pl.semaphore_signal(barrier, inc=1, device_id=peer, device_id_type=MESH)

    lane = lax.broadcasted_iota(jnp.int32, (LANES, LANES), 1)
    get_echo.wait()
    for v in range(nlane):
        total = jnp.zeros((LANES, LANES), F32)
        for c in range(2):
            for q in range(chunks):
                part = echo[core, c, v * LANES : (v + 1) * LANES, q * LANES : (q + 1) * LANES].astype(F32)
                total = total + part * part
        power[4, v : v + 1, :] = jnp.sum(total.T, axis=0, keepdims=True)

    lane_f = lane.astype(F32)

    def one_hot_block(b):
        col = cols[b]
        return [(col == lane_f + float(w * LANES)) for w in range(blocks)]

    def permuted(b):
        hot = jnp.concatenate([m.astype(F32).astype(BF16) for m in one_hot_block(b)], axis=1)
        left = jnp.dot(hot, steer[0], preferred_element_type=F32)
        right = jnp.dot(hot, steer[1], preferred_element_type=F32)
        return left.astype(BF16), right.astype(BF16)

    def permute(target, side, first, last):
        @pl.loop(first, last)
        def _(i):
            dest = i // half_blocks
            u = lax.rem(i, half_blocks)
            left, right = permuted((dest * 2 + side) * half_blocks + u)
            rows = pl.ds(pl.multiple_of(u * LANES, LANES), LANES)
            target[dest, rows, :chans] = left
            target[dest, rows, chans:] = right

    small[0].wait()
    order_cols = order_ref[...].astype(F32)
    for b in range(blocks):
        cols[b] = jnp.broadcast_to(order_cols[b : b + 1, :], (LANES, LANES)).T
    get_steer.wait()
    permute(perm_out, 1 - core, 0, half_blocks)
    pl.semaphore_wait(barrier, len(greeted))

    for d in (-4, 4, -3, 3, -2, 2, -1, 1):
        pltpu.make_async_remote_copy(
            power.at[4], power.at[4 - d], ar_send.at[0], ar_recv.at[0],
            device_id=at(tile, my_y, zs(d)), device_id_type=MESH,
        ).start()

    send_echo = pltpu.make_async_remote_copy(
        echo.at[core], echo.at[core], pair_send.at[0], pair_recv.at[0],
        device_id={"tile": other}, device_id_type=MESH,
    )
    send_echo.start()
    permute(perm_out, 1 - core, half_blocks, 4 * half_blocks)
    send_perm = pltpu.make_async_remote_copy(
        perm_out, perm.at[core], pair_send.at[1], pair_recv.at[1],
        device_id={"tile": other}, device_id_type=MESH,
    )
    send_perm.start()
    nearby = power.at[pl.ds(0, 8)]
    pltpu.make_async_copy(nearby, nearby, ar_recv.at[0]).wait()
    around = jnp.sum(power[...], axis=0)
    stage[0] = around
    stage[1] = jnp.sum(power[5:9], axis=0)
    stage[2] = jnp.sum(power[1:4], axis=0)
    gathered[(core * 3) * ny + my_y] = around
    for kind, d in ((1, -4), (2, 4), (0, 0)):
        for step, y in enumerate(ys):
            for side in (tile, other):
                if kind == 0 and step == 0 and side is tile:
                    continue
                pltpu.make_async_remote_copy(
                    stage.at[kind], gathered.at[(core * 3 + kind) * ny + my_y], ar_send.at[1], ar_recv.at[1],
                    device_id=at(side, y, zs(d)), device_id_type=MESH,
                ).start()
    permute(perm.at[core], core, 0, 4 * half_blocks)

    for copy in small[1:]:
        copy.wait()
    taps = code_ref[...].astype(F32)
    for tap in range(TAPS):
        for c in range(2):
            coef[2 * tap + c] = jnp.broadcast_to(taps[c : c + 1, tap : tap + 1], coef.shape[1:])

    for u in range(half_blocks):
        masks = one_hot_block(tile * half_blocks + u)
        length = jnp.zeros((LANES, LANES), F32)
        keep = jnp.zeros((LANES, LANES), F32)
        for w in range(blocks):
            length = length + jnp.where(masks[w], lens_ref[w : w + 1, :].astype(F32), 0.0)
            keep = keep + jnp.where(masks[w], dwell_ref[w : w + 1, :].astype(F32), 0.0)
        length = jnp.sum(length, axis=1, keepdims=True)
        keep = jnp.sum(keep, axis=1, keepdims=True)
        gate = lax.rem(lane, G).astype(F32)
        limit[u * LANES : (u + 1) * LANES, :] = jnp.minimum(jnp.broadcast_to(length, (LANES, LANES)), G - gate)
        first = (lane // G + beam * (chunks * (LANES // G))).astype(F32)
        pulses[u * LANES : (u + 1) * LANES, :] = jnp.broadcast_to(keep, (LANES, LANES)) - first

    everyone = gathered.at[pl.ds(0, 6 * ny - 1)]
    pltpu.make_async_copy(everyone, everyone, ar_recv.at[1]).wait()
    for side in range(2):
        total = jnp.sum(gathered[side * 3 * ny : (side + 1) * 3 * ny], axis=0)
        gains[side] = lax.rsqrt(total * (1.0 / (nb * chunks * LANES)) + 1e-05)

    def spread_gain(side):
        for v in range(nlane):
            spread[side, v] = jnp.broadcast_to(gains[side, v : v + 1, :], (LANES, LANES)).T

    def scale(side, q):
        for v in range(nlane):
            gain = spread[side, v]
            top = slice(v * LANES, (v + 1) * LANES)
            low = slice(chans + v * LANES, chans + (v + 1) * LANES)
            span = slice(q * LANES, (q + 1) * LANES)
            real = (echo[side, 0, top, span].astype(F32) * gain).astype(BF16)
            imag = (echo[side, 1, top, span].astype(F32) * gain).astype(BF16)
            rhs[q, side, top, :LANES] = real
            rhs[q, side, low, :LANES] = -imag
            rhs[q, side, top, LANES:] = imag
            rhs[q, side, low, LANES:] = real

    send_echo.wait_recv()
    send_perm.wait_recv()
    spread_gain(0)
    spread_gain(1)

    def partial_beams(q, dest):
        return jnp.dot(perm[0, dest], rhs[q, 0], preferred_element_type=F32) + jnp.dot(
            perm[1, dest], rhs[q, 1], preferred_element_type=F32
        )

    units = [(0, (k,)) for k in range(ny)] + [(q, tuple(range(ny))) for q in range(1, chunks)]
    places = [lax.rem(y + ny - my_y, ny) for y in range(ny)]
    block = (ny, 2, slots // (2 * ny), 2 * LANES)
    x_copies = []

    def to_chip(chip, source, target, sent, received):
        copy = pltpu.make_async_remote_copy(
            source, target, sent, received, device_id={"tile": 2 * chip + core}, device_id_type=MESH
        )
        copy.start()
        x_copies.append(copy)
        return copy

    far, near = {}, {}

    def start_far(n):
        q, steps = units[n]
        span = pl.ds(steps[0], len(steps))
        for side in range(2):
            far[n, side] = to_chip(
                across if n == 0 else sides[side], far_out.at[q, side, span], far_in.at[q, side, span],
                far_send.at[n, side], far_recv.at[n, side],
            )

    def start_near(n, side, part, which):
        q, steps = units[n]
        span = pl.ds(steps[0], len(steps))
        near[n, side, which] = to_chip(
            sides[side], near_out.at[q, side, part, span], near_in.at[q, side, part, span],
            near_send.at[n, side, which], near_recv.at[n, side, which],
        )

    def form_far(q):
        product = partial_beams(q, across).reshape(block)
        for y in range(ny):
            for side in range(2):
                far_out[q, side, places[y]] = product[y, side].astype(BF16)

    def form_near(q, side):
        product = partial_beams(q, sides[side]).reshape(block)
        for y in range(ny):
            near_out[q, side, 1 - side, places[y]] = product[y, 1 - side].astype(BF16)
            hold[q, side, places[y]] = product[y, side]
            if q == 0:
                near_out[q, side, side, places[y]] = product[y, side].astype(BF16)

    def form_own(q):
        product = partial_beams(q, chip_x).reshape(block)
        for y in range(ny):
            own[q, places[y]] = product[y].reshape(slots // ny, 2 * LANES)

    def relay(n):
        q, steps = units[n]
        for side in range(2):
            far[n, side].wait_recv()
            for k in steps:
                near_out[q, side, side, k] = (hold[q, side, k] + far_in[q, side, k].astype(F32)).astype(BF16)
            start_near(n, side, side, 1)

    step = slots // ny

    def finish(n):
        q, steps = units[n]
        for side in range(2):
            for which in range(2):
                near[n, side, which].wait_recv()
            if n == 0:
                far[n, side].wait_recv()

        def block_of(k, y):
            rows = pl.ds(pl.multiple_of(y * step, step), step)
            both = own[q, k]
            for side in range(2):
                both = both + jnp.concatenate(
                    [near_in[q, side, part, k].astype(F32) for part in range(2)], axis=0
                )
            if n == 0:
                both = both + jnp.concatenate([far_in[q, part, k].astype(F32) for part in range(2)], axis=0)
            tiled = (step // 8, 8, LANES)
            real, imag = both[:, :LANES].reshape(tiled), both[:, LANES:].reshape(tiled)
            cut = limit[rows, :].reshape(tiled)
            out_re = jnp.zeros(tiled, F32)
            out_im = jnp.zeros(tiled, F32)
            for tap in range(TAPS):
                live = cut > float(tap)
                shift_re = real if tap == 0 else pltpu.roll(real, LANES - tap, 2)
                shift_im = imag if tap == 0 else pltpu.roll(imag, LANES - tap, 2)
                shift_re = jnp.where(live, shift_re, 0.0)
                shift_im = jnp.where(live, shift_im, 0.0)
                code_re = coef[2 * tap]
                code_im = coef[2 * tap + 1]
                out_re = out_re + (code_re * shift_re + code_im * shift_im)
                out_im = out_im + (code_re * shift_im - code_im * shift_re)
            kept = pulses[rows, :].reshape(tiled) > float(q * (LANES // G))
            weave[k, pl.ds(0, step, stride=2), :] = jnp.where(kept, out_re, 0.0).reshape(step, LANES)
            weave[k, pl.ds(1, step, stride=2), :] = jnp.where(kept, out_im, 0.0).reshape(step, LANES)
            zsend[q, k] = weave[k].reshape(zsend.shape[2:]).astype(BF16)

        if len(steps) == 1:
            block_of(steps[0], ys[steps[0]])
        else:

            @pl.loop(0, ny)
            def _(k):
                block_of(k, lax.rem(my_y + k, ny))

        start_plane_sends(q, steps)
        if 0 in steps:
            pltpu.make_async_copy(zsend.at[q, 0, my_z], zrecv.at[q, beam], self_sem.at[q]).start()

    scale(0, 0)
    scale(1, 0)
    form_far(0)
    for n in range(ny):
        start_far(n)
    for side in range(2):
        form_near(0, side)
        start_near(0, side, 1 - side, 0)
        start_near(0, side, side, 1)
    for side in range(2):
        for n in range(1, ny):
            start_near(n, side, 1 - side, 0)
    def form_rest(q):
        scale(0, q)
        scale(1, q)
        form_far(q)
        form_near(q, 0)
        form_near(q, 1)
        form_own(q)

    def start_rest(n):
        start_far(n)
        for side in range(2):
            start_near(n, side, 1 - side, 0)

    form_own(0)
    form_rest(1)
    form_rest(2)
    form_rest(3)
    for n in range(1, ny):
        relay(n)
    start_rest(ny)
    for n in range(ny):
        finish(n)
    for n in range(ny, len(units)):
        relay(n)
        if n + 1 < len(units):
            start_rest(n + 1)
        finish(n)

    for q in range(chunks):
        arrived = zrecv.at[q, pl.ds(0, nb - 1)]
        pltpu.make_async_copy(arrived, arrived, z_recv.at[q]).wait()
        pltpu.make_async_copy(zsend.at[q, 0, my_z], zrecv.at[q, beam], self_sem.at[q]).wait()
        wide[...] = zrecv[q].astype(F32).reshape(wide.shape)
        for slot in range(4):
            pair = [wide[pl.ds(2 * slot + c, nb, stride=8), :] for c in range(2)]
            out_ref[slot, :, q * LANES : (q + 1) * LANES] = jnp.concatenate(pair, axis=0).T.astype(BF16)

    pltpu.make_async_copy(nearby, nearby, ar_send.at[0]).wait()
    pltpu.make_async_copy(everyone, everyone, ar_send.at[1]).wait()
    send_echo.wait_send()
    send_perm.wait_send()
    for copy in x_copies:
        copy.wait_send()
    for q in range(chunks):
        sent = zrecv.at[q, pl.ds(0, nb - 1)]
        pltpu.make_async_copy(sent, sent, z_send.at[q]).wait()


def exchange(nb, echoes, steer, code, beam_order, dwell, code_len):
    chans, columns = echoes.shape[1], echoes.shape[2]
    total = steer.shape[1]
    slots = total // 8
    chunks = columns // LANES
    units = chunks + 3
    blocks = total // LANES
    vmem = pl.BlockSpec(memory_space=pltpu.VMEM)
    hbm = pl.BlockSpec(memory_space=pltpu.HBM)
    dma = pltpu.SemaphoreType.DMA

    def body(*refs):
        exchange_kernel(nb, *refs)

    return pl.pallas_call(
        body,
        out_shape=jax.ShapeDtypeStruct((slots // nb, LANES, 2 * nb * chunks), BF16),
        in_specs=[hbm] * 6,
        out_specs=vmem,
        scratch_shapes=[
            pltpu.VMEM((blocks, LANES), jnp.int32),
            pltpu.VMEM((blocks, LANES), jnp.int32),
            pltpu.VMEM((blocks, LANES), jnp.int32),
            pltpu.VMEM(code.shape, BF16),
            pltpu.VMEM((2 * TAPS, 8, LANES), F32),
            pltpu.VMEM((2, 2, chans, columns), BF16),
            pltpu.VMEM(steer.shape, BF16),
            pltpu.VMEM((blocks, LANES, LANES), F32),
            pltpu.VMEM((2, 4, slots, 2 * chans), BF16),
            pltpu.VMEM((4, slots, 2 * chans), BF16),
            pltpu.VMEM((9, chans // LANES, LANES), F32),
            pltpu.VMEM((3, chans // LANES, LANES), F32),
            pltpu.VMEM((24, chans // LANES, LANES), F32),
            pltpu.VMEM((2, chans // LANES, LANES), F32),
            pltpu.VMEM((2, chans // LANES, LANES, LANES), F32),
            pltpu.VMEM((slots, LANES), F32),
            pltpu.VMEM((slots, LANES), F32),
            pltpu.VMEM((chunks, 2, 2 * chans, 2 * LANES), BF16),
            pltpu.VMEM((chunks, 2, 4, slots // 8, 2 * LANES), BF16),
            pltpu.VMEM((chunks, 2, 4, slots // 8, 2 * LANES), BF16),
            pltpu.VMEM((chunks, 2, 2, 4, slots // 8, 2 * LANES), BF16),
            pltpu.VMEM((chunks, 2, 2, 4, slots // 8, 2 * LANES), BF16),
            pltpu.VMEM((chunks, 2, 4, slots // 8, 2 * LANES), F32),
            pltpu.VMEM((chunks, 4, slots // 4, 2 * LANES), F32),
            pltpu.VMEM((4, slots // 2, LANES), F32),
            pltpu.VMEM((chunks, 4, nb // 4, 8, LANES), BF16),
            pltpu.VMEM((chunks, nb, 8, LANES), BF16),
            pltpu.VMEM((nb * 8, LANES), F32),
            dma((6,)), dma((2,)), dma((2,)), dma((2,)), dma((2,)),
            dma((units, 2)), dma((units, 2)), dma((units, 2, 2)), dma((units, 2, 2)), dma((chunks,)), dma((chunks,)), dma((chunks,)),
        ],
        compiler_params=pltpu.CompilerParams(
            collective_id=0, has_side_effects=True, vmem_limit_bytes=40 << 20
        ),
        name="exchange",
    )(
        *[
            pltpu.with_memory_space_constraint(x, pltpu.HBM)
            for x in (
                echoes, steer,
                beam_order.reshape(blocks, LANES), dwell.reshape(blocks, LANES), code_len.reshape(blocks, LANES),
                code,
            )
        ]
    )


def dft_tables(nb, chunks, pulses_all):
    length = nb * chunks
    radix = pulses_all // length
    index = np.arange(nb)[None, :] * chunks + np.arange(chunks)[:, None]
    angle = -2.0 * np.pi * ((index[:, :, None] * np.arange(length)) % length) / length
    real, imag = np.cos(angle), np.sin(angle)
    table = np.concatenate(
        [np.concatenate([real, imag], axis=2), np.concatenate([-imag, real], axis=2)], axis=1
    ).reshape(2 * length, 2 * length)
    turn = -2.0 * np.pi * np.arange(radix)[:, None] * np.arange(length)[None, :] / pulses_all
    twist = np.concatenate([np.cos(turn), np.sin(turn)], axis=0) / math.sqrt(pulses_all)
    return jnp.asarray(table, BF16), jnp.asarray(twist, F32)


def dft_slot(x_ref, table_ref, twist_ref, out_ref):
    length = x_ref.shape[1] // 2
    found = jnp.dot(x_ref[...], table_ref[...], preferred_element_type=F32)
    re, im = [], []
    for p in range(4):
        fr = found[p * G : (p + 1) * G, :length]
        fi = found[p * G : (p + 1) * G, length:]
        wr = twist_ref[p : p + 1, :]
        wi = twist_ref[4 + p : 5 + p, :]
        re.append(fr * wr - fi * wi)
        im.append(fr * wi + fi * wr)
    even_re, even_im = re[0] + re[2], im[0] + im[2]
    odd_re, odd_im = re[0] - re[2], im[0] - im[2]
    side_re, side_im = re[1] + re[3], im[1] + im[3]
    turn_re, turn_im = re[1] - re[3], im[1] - im[3]
    parts = [
        (even_re + side_re, even_im + side_im),
        (odd_re + turn_im, odd_im - turn_re),
        (even_re - side_re, even_im - side_im),
        (odd_re - turn_im, odd_im + turn_re),
    ]
    for k, (a, b) in enumerate(parts):
        out_ref[0, :, k * length : (k + 1) * length] = a
        out_ref[1, :, k * length : (k + 1) * length] = b


def dft_kernel(x_ref, table_ref, twist_ref, out_ref):
    for n in range(out_ref.shape[0]):
        dft_slot(x_ref.at[pl.program_id(0) * out_ref.shape[0] + n], table_ref, twist_ref, out_ref.at[n])


def doppler(x, nb, pulses_all):
    slots, _, width = x.shape
    table, twist = dft_tables(nb, width // (2 * nb), pulses_all)
    vmem = pl.BlockSpec(memory_space=pltpu.VMEM)
    return pl.pallas_call(
        dft_kernel,
        grid=(slots // 2,),
        out_shape=jax.ShapeDtypeStruct((slots, 2, G, pulses_all), F32),
        in_specs=[vmem, vmem, vmem],
        out_specs=pl.BlockSpec((2, 2, G, pulses_all), lambda n: (n, 0, 0, 0)),
        compiler_params=pltpu.CompilerParams(vmem_limit_bytes=8 << 20),
        name="doppler",
    )(x, table, twist)


def solution(mesh):
    nb = mesh.shape["beam"]

    def on_device(echoes, steer, code, beam_order, dwell, code_len):
        arrived = exchange(nb, echoes, steer, code, beam_order, dwell, code_len)
        return doppler(arrived, nb, nb * echoes.shape[2] // G)

    placed = (P(None, "tile", "beam"), P(None, None, "tile"), P(), P(), P(), P())
    return jax.shard_map(
        on_device,
        mesh=mesh,
        in_specs=placed,
        out_specs=P(("tile", "beam"), None, None, None),
        check_vma=False,
    )
```
